512 devices in a mesh: row: 32 (over z, y_hi), col: 16 (over y_lo, x, core).
Axes of the slice: x: 4, y: 4 (y_hi: 2, y_lo: 2; y = y_hi * 2 + y_lo), z: 16, core: 2. Of those that a mesh axis runs over, the one named last changes fastest.
Arguments:
- z_trunk: bfloat16 [2048, 2048, 128], P('row', 'col'), may hold values from -6 to 6
- chain_id: int32 [2048], replicated, may hold values from 0 to 5, never falling along the last dimension, each value on 1 to 512 neighbouring positions
- residue: int32 [2048], replicated, may hold values from 0 to 47
- single: bfloat16 [2048, 768], P(('row', 'col')), may hold values from -6 to 6
- gain_single: float32 [768], replicated, may hold values from 0.1 to 1.9
- w_proj: bfloat16 [768, 3072], P(None, ('row', 'col')), may hold values from -8 to 8
- w_out: bfloat16 [768, 768], replicated, may hold values from -0.21875 to 0.21875
- gain_trunk: float32 [128], replicated, may hold values from 0.1 to 1.9
- w_pair: bfloat16 [128, 128], replicated, may hold values from -0.5 to 0.5
- rel_table: bfloat16 [71, 128], replicated, may hold values from -5 to 5
- gain_trans: float32 [2, 128], replicated, may hold values from 0.1 to 1.9
- w_up: bfloat16 [2, 128, 512], replicated, may hold values from -0.5 to 0.5
- w_down: bfloat16 [2, 256, 128], replicated, may hold values from -0.375 to 0.375
- gain_bias: float32 [128], replicated, may hold values from 0.1 to 1.9
- w_bias: bfloat16 [128, 16], replicated, may hold values from -2 to 2
Outputs:
- update: bfloat16 [2048, 768], P(('row', 'col'))
The draws below stay inside these ranges and needn't reach their ends.
Inputs may be any that keep to these rules, and one draw needn't show every extreme that they name: `chain_id`: chain numbers never fall along the tokens.
All inputs are finite; a program needn't handle non-finite values.
Results may differ from the reference program's by a relative error of at most 0.039.
Values may be sent and summed in bfloat16 or wider, within the bound.
A program may use at most 64 MiB of HBM per device.

```python
import math
import jax
import jax.numpy as jnp
import numpy as np
from jax import lax

D = 768
HEADS = 16
CZ = 128
HID = 256
TRANS = 2
RMAX = 32
CMAX = 2
Q_DEV = 64
N = 2048


def draw_w_proj(key, part):
    base = jax.random.normal(key, (D, 4 * D), jnp.float32) * (1.0 / jnp.sqrt(jnp.float32(D)))
    return jnp.clip(base, -8.0, 8.0).astype(jnp.bfloat16)


def set_ends(drawn, stream_key, least, top_value):
    index_at = [jax.random.randint(jax.random.fold_in(stream_key, axis), (), 0, length) for axis, length in enumerate(drawn.shape)]
    widest = drawn.shape.index(max(drawn.shape))
    next_to = index_at[:widest] + [(index_at[widest] + 1) % drawn.shape[widest]] + index_at[widest + 1:]
    return drawn.at[tuple(index_at)].set(least).at[tuple(next_to)].set(top_value)


def block_levels(key, extent, pieces, low, top_value):
    loudness = 1.0
    for position, shards_of in pieces:
        steps = jax.random.uniform(jax.random.fold_in(jax.random.fold_in(key, 6), position), (shards_of,), jnp.float32, low / len(pieces), top_value / len(pieces))
        loudness = loudness * jnp.repeat(jnp.exp(steps), extent[position] // shards_of).reshape((-1,) + (1,) * (len(extent) - 1 - position))
    return loudness


def profile(amount, total, reach, slope):
    portions = [(1 << 20) // math.isqrt(grade ** slope) + 1 for grade in range(2, amount + 1)]
    surplus, counts = total - reach - (amount - 1), [1] * (amount - 1)
    while surplus > 0:
        movable = [i for i in range(amount - 1) if counts[i] < reach]
        mass, budget = sum([portions[i] for i in movable]), surplus
        for i in movable:
            addition = min(reach - counts[i], max(1, budget * portions[i] // mass), surplus)
            counts[i] = counts[i] + addition
            surplus = surplus - addition
    return np.array([reach] + counts)


def ragged_sizes(rng, amount, total, reach, lean):
    if amount == 2:
        one = jax.random.randint(rng, (), max(1, total - reach), min(reach, total - 1) + 1)
        return jnp.stack([one, total - one])
    lengths = jnp.asarray(profile(amount, total, reach, lean), jnp.int32)
    couples = (amount - 1) // 2
    giver, receiver = lengths[1:1 + 2 * couples:2], lengths[2:2 + 2 * couples:2]
    slack = jnp.minimum(giver - 1, reach - receiver)
    passed = jax.random.randint(jax.random.fold_in(rng, 1), (couples,), 0, 1 << 20) % (slack + 1)
    lengths = lengths.at[1:1 + 2 * couples:2].set(giver - passed).at[2:2 + 2 * couples:2].set(receiver + passed)
    return lengths[jax.random.permutation(jax.random.fold_in(rng, 2), amount)]


def gaussian(key, shape, scale, bound, split=(), kind=jnp.bfloat16):
    result = scale * jax.random.normal(key, shape, jnp.float32)
    if split:
        result = result * block_levels(key, shape, split, -0.22, 0.18)
    return jnp.clip(result, -bound, bound).astype(kind)


def setup_inputs(seed: int = 0) -> dict:
    arg_keys = jax.random.split(jax.random.key(seed), 16)
    return {
        "z_trunk": gaussian(arg_keys[0], (N, N, CZ), 1.0, 6.0, ((0, 32), (1, 16))),
        "chain_id": jnp.searchsorted(jnp.cumsum(ragged_sizes(arg_keys[1], 6, N, N // 4, 1)), jnp.arange(N), side="right").astype(jnp.int32),
        "residue": set_ends(jax.random.randint(arg_keys[2], (N,), 0, 48), jax.random.fold_in(arg_keys[2], 1), 0, 47).astype(jnp.int32),
        "single": gaussian(arg_keys[3], (N, D), 1.0, 6.0, ((0, 512),)),
        "gain_single": jnp.clip(1.0 + 0.18 * jax.random.normal(arg_keys[4], (D,), jnp.float32), 0.1, 1.9),
        "w_proj": draw_w_proj(jax.random.fold_in(arg_keys[15], 71), 0),
        "w_out": gaussian(arg_keys[6], (D, D), D ** -0.5, 0.21875),
        "gain_trunk": jnp.clip(1.0 + 0.18 * jax.random.normal(arg_keys[7], (CZ,), jnp.float32), 0.1, 1.9),
        "w_pair": gaussian(arg_keys[8], (CZ, CZ), CZ ** -0.5, 0.5),
        "rel_table": gaussian(arg_keys[9], (2 * RMAX + 2 * CMAX + 3, CZ), 1.0, 5.0),
        "gain_trans": jnp.clip(1.0 + 0.18 * jax.random.normal(arg_keys[10], (TRANS, CZ), jnp.float32), 0.1, 1.9),
        "w_up": gaussian(arg_keys[11], (TRANS, CZ, 2 * HID), CZ ** -0.5, 0.5),
        "w_down": gaussian(arg_keys[12], (TRANS, HID, CZ), HID ** -0.5, 0.375),
        "gain_bias": jnp.clip(1.0 + 0.18 * jax.random.normal(arg_keys[13], (CZ,), jnp.float32), 0.1, 1.9),
        "w_bias": gaussian(arg_keys[14], (CZ, HEADS), (CZ // 16) ** -0.5, 2.0),
    }


def layer_norm(values, gain):
    values = values.astype(jnp.float32)
    center = values - lax.optimization_barrier(jnp.mean(values, axis=-1, keepdims=True))
    spread = lax.optimization_barrier(jnp.mean(center * center, axis=-1, keepdims=True))
    return center * lax.rsqrt(spread + 1e-05) * gain

def pair_bias(pair_in, chain_q, res_q, chain_k, res_k, gain_trunk, w_pair, rel_table, gain_trans, w_up, w_down, gain_bias, w_bias):
    same_chain = chain_q[:, None] == chain_k[None, :]
    res_bin = jnp.where(same_chain, jnp.clip(res_q[:, None] - res_k[None, :], -RMAX, RMAX) + RMAX, 2 * RMAX + 1)
    chain_bin = jnp.clip(chain_q[:, None] - chain_k[None, :], -CMAX, CMAX) + 2 * RMAX + 2
    bins = jnp.arange(rel_table.shape[0], dtype=jnp.int32)
    one_hot = ((res_bin[..., None] == bins) | (chain_bin[..., None] == bins)).astype(jnp.bfloat16)
    width = pair_in.shape[-1]
    flat = pair_in.reshape(-1, width)
    one_hot = one_hot.reshape(flat.shape[0], -1)
    normed = layer_norm(flat, gain_trunk).astype(jnp.bfloat16)
    pair = (jnp.dot(normed, w_pair, preferred_element_type=jnp.float32) + jnp.dot(one_hot, rel_table, preferred_element_type=jnp.float32)).astype(jnp.bfloat16)
    hidden = w_down.shape[1]
    for layer in range(w_up.shape[0]):
        normed = layer_norm(pair, gain_trans[layer]).astype(jnp.bfloat16)
        expanded = jnp.dot(normed, w_up[layer], preferred_element_type=jnp.float32)
        swiglu = (jax.nn.silu(expanded[:, :hidden]) * expanded[:, hidden:]).astype(jnp.bfloat16)
        pair = (pair.astype(jnp.float32) + jnp.dot(swiglu, w_down[layer], preferred_element_type=jnp.float32)).astype(jnp.bfloat16)
    bias_normed = layer_norm(pair, gain_bias).astype(jnp.bfloat16)
    bias = jnp.dot(bias_normed, w_bias, preferred_element_type=jnp.float32)
    return bias.reshape(pair_in.shape[0], pair_in.shape[1], -1)

def reference(z_trunk, chain_id, residue, single, gain_single, w_proj, w_out, gain_trunk, w_pair, rel_table, gain_trans, w_up, w_down, gain_bias, w_bias):
    width = single.shape[1]
    heads = w_bias.shape[1]
    head_dim = width // heads
    total = single.shape[0]
    normed = layer_norm(single, gain_single).astype(jnp.bfloat16)
    projected = jnp.dot(normed, w_proj, preferred_element_type=jnp.float32)
    queries = projected[:, :width].astype(jnp.bfloat16)
    keys = projected[:, width:2 * width].astype(jnp.bfloat16)
    values = projected[:, 2 * width:3 * width].astype(jnp.bfloat16)
    gating = jax.nn.sigmoid(projected[:, 3 * width:])
    keys3 = keys.reshape(total, heads, head_dim).astype(jnp.float32)
    values3 = values.reshape(total, heads, head_dim).astype(jnp.float32)

    def one_block(block):
        start = (block * Q_DEV).astype(jnp.int32)
        pair_in = lax.dynamic_slice_in_dim(z_trunk, start, Q_DEV, 0)
        chain_q = lax.dynamic_slice_in_dim(chain_id, start, Q_DEV, 0)
        res_q = lax.dynamic_slice_in_dim(residue, start, Q_DEV, 0)
        bias = pair_bias(pair_in, chain_q, res_q, chain_id, residue, gain_trunk, w_pair, rel_table, gain_trans, w_up, w_down, gain_bias, w_bias)
        query_blk = lax.dynamic_slice_in_dim(queries, start, Q_DEV, 0).reshape(Q_DEV, heads, head_dim).astype(jnp.float32)
        scores = jnp.einsum('qhd,khd->hqk', query_blk, keys3) / jnp.sqrt(jnp.float32(head_dim)) + jnp.transpose(bias, (2, 0, 1))
        peak = lax.optimization_barrier(jnp.max(scores, axis=-1, keepdims=True))
        expo = jnp.exp(scores - peak)
        totals = lax.optimization_barrier(jnp.sum(expo, axis=-1))
        weights = expo.astype(jnp.bfloat16).astype(jnp.float32)
        summed = jnp.einsum('hqk,khd->qhd', weights, values3)
        gate_blk = lax.dynamic_slice_in_dim(gating, start, Q_DEV, 0)
        attended = ((summed / jnp.transpose(totals)[:, :, None]).reshape(Q_DEV, width) * gate_blk).astype(jnp.bfloat16)
        return jnp.dot(attended, w_out, preferred_element_type=jnp.float32).astype(jnp.bfloat16)
    blocks = lax.map(one_block, jnp.arange(total // Q_DEV, dtype=jnp.int32))
    return blocks.reshape(total, width)
```

```python
import functools

import jax
import jax.numpy as jnp
import numpy as np
from jax import lax
from jax.experimental import pallas as pl
from jax.experimental.pallas import tpu as pltpu
from jax.sharding import PartitionSpec as P

NT = (((1,), (1,)), ((), ()))
F32 = jnp.float32
BF16 = jnp.bfloat16
BIG = 1 << 20
QB = 32


def norm_cols(values):
    center = values - jnp.mean(values, axis=0, keepdims=True)
    spread = jnp.mean(center * center, axis=0, keepdims=True)
    return (center * lax.rsqrt(spread + 1e-05)).astype(BF16)


def interval_bounds(chain_k, res_k):
    bins = lax.broadcasted_iota(jnp.int32, (128, 128), 0)
    base = jnp.broadcast_to(chain_k * 64, (128, 128))
    res = jnp.broadcast_to(res_k, (128, 128))
    shifted = res + bins - 32
    inside = (shifted >= 0) & (shifted <= 63)
    low = jnp.where(inside, base + shifted, BIG)
    high = jnp.where(inside, base + shifted, -BIG)

    def put(low, high, index, new_low, new_high):
        hit = bins == index
        return jnp.where(hit, new_low, low), jnp.where(hit, new_high, high)

    low, high = put(low, high, 0, base, base + res - 32)
    low, high = put(low, high, 64, base + res + 32, base + 63)
    low, high = put(low, high, 65, jnp.full_like(base, -BIG), base - 1)
    low, high = put(low, high, 66, base, base + 63)
    low, high = put(low, high, 67, base + 64, base + 127)
    low, high = put(low, high, 68, base + 128, jnp.full_like(base, BIG))
    low, high = put(low, high, 69, jnp.full_like(base, -BIG), base - 65)
    low, high = put(low, high, 70, base + 64, jnp.full_like(base, BIG))
    unused = bins > 70
    return jnp.where(unused, BIG, low), jnp.where(unused, -BIG, high)


def bias_kernel(
    chain_sm, res_sm, z_ref, chain_ref, res_ref, gtrunk_ref, wpair_ref, rel_ref, gtrans_ref,
    wup_ref, wdown_ref, gbias_ref, wbias_ref, out_ref, low_ref, high_ref, wcat, wup, wdn, wb, rel,
):
    step = pl.program_id(0)
    row_pos = lax.axis_index("row")
    col_pos = lax.axis_index("col")

    @pl.when(step == 0)
    def _():
        low, high = interval_bounds(chain_ref[pl.ds(col_pos, 1), :], res_ref[pl.ds(col_pos, 1), :])
        low_ref[...] = low
        high_ref[...] = high
        wcat[:, :128] = (wpair_ref[...].astype(F32).T * gtrunk_ref[...]).astype(BF16)
        rel[...] = jnp.zeros_like(rel)
        rel[0:69, :] = rel_ref[0:69, :].astype(F32)
        rel[69:70, :] = rel_ref[64:65, :].astype(F32)
        rel[70:71, :] = rel_ref[65:66, :].astype(F32)
        wcat[:, 128:] = rel[...].T.astype(BF16)
        for t in range(2):
            up = wup_ref[t].astype(F32).T * gtrans_ref[t : t + 1, :]
            wup[t, :256] = (up[:256] * 0.5).astype(BF16)
            wup[t, 256:] = up[256:].astype(BF16)
            wdn[t] = wdown_ref[t].astype(F32).T.astype(BF16)
        wb[...] = (wbias_ref[...].astype(F32).T * gbias_ref[...]).astype(BF16)

    low = low_ref[...]
    high = high_ref[...]
    tiles = [z_ref[j].astype(F32).T for j in range(QB)]
    normed = norm_cols(jnp.concatenate(tiles, axis=1))
    hots = []
    for j in range(QB):
        token = row_pos * 64 + step * QB + j
        code = chain_sm[token] * 64 + res_sm[token]
        hots.append(jnp.where((low <= code) & (high >= code), 1.0, 0.0).astype(BF16))
    both = jnp.concatenate([normed, jnp.concatenate(hots, axis=1)], axis=0)
    pair = jnp.dot(wcat[...], both, preferred_element_type=F32)
    for t in range(2):
        expanded = jnp.dot(wup[t], norm_cols(pair), preferred_element_type=F32)
        half = expanded[:256]
        product = half * expanded[256:]
        swiglu = (product + product * jnp.tanh(half)).astype(BF16)
        pair = pair + jnp.dot(wdn[t], swiglu, preferred_element_type=F32)
    bias = jnp.dot(wb[...], norm_cols(pair), preferred_element_type=F32)
    for j in range(QB):
        out_ref[j] = bias[:, j * 128 : (j + 1) * 128]


def pair_bias(z, chain_id, residue, gain_trunk, w_pair, rel_table, gain_trans, w_up, w_down, gain_bias, w_bias):
    def full(*shape):
        return pl.BlockSpec(shape, lambda i, *_: (0,) * len(shape))

    spec = pltpu.PrefetchScalarGridSpec(
        num_scalar_prefetch=2,
        grid=(64 // QB,),
        in_specs=[
            pl.BlockSpec((QB, 128, 128), lambda i, *_: (i, 0, 0)),
            full(16, 128), full(16, 128), full(1, 128), full(128, 128), full(71, 128), full(2, 128),
            full(2, 128, 512), full(2, 256, 128), full(1, 128), full(128, 16),
        ],
        out_specs=pl.BlockSpec((QB, 16, 128), lambda i, *_: (i, 0, 0)),
        scratch_shapes=[
            pltpu.VMEM((128, 128), jnp.int32),
            pltpu.VMEM((128, 128), jnp.int32),
            pltpu.VMEM((128, 256), BF16),
            pltpu.VMEM((2, 512, 128), BF16),
            pltpu.VMEM((2, 128, 256), BF16),
            pltpu.VMEM((16, 128), BF16),
            pltpu.VMEM((128, 128), F32),
        ],
    )
    return pl.pallas_call(
        bias_kernel,
        grid_spec=spec,
        out_shape=jax.ShapeDtypeStruct((64, 16, 128), F32),
        compiler_params=pltpu.CompilerParams(vmem_limit_bytes=60 << 20),
    )(
        chain_id, residue, z, chain_id.reshape(16, 128), residue.reshape(16, 128), gain_trunk.reshape(1, 128),
        w_pair, rel_table, gain_trans, w_up, w_down, gain_bias.reshape(1, 128), w_bias,
    )


def orders():
    natural = np.zeros(768, np.int64)
    for g in range(32):
        for zk in range(4):
            for i in range(6):
                natural[g * 24 + zk * 6 + i] = 192 * zk + 6 * g + i
    heads = np.zeros((128, 768), np.float32)
    heads[natural // 48, np.arange(768)] = 1.0
    perm = np.zeros((768, 768), np.float32)
    perm[np.arange(768), natural] = 1.0
    return heads, perm


def main_kernel(
    x_ref, gain_ref, wt_ref, heads_ref, bias_hbm, wout_hbm, perm_hbm, out_ref,
    xs, xg, wg, xf, wf, kvs, qgs, kvz, kvb, qgb, tf, kt, vt, qf, gate, bias, wout, perm, woutp,
    o_src, o_all, st_src, st_all, fac,
    local_sem, w_send, w_recv, x_send, x_recv, qg_send, qg_recv, kz_send, kz_recv, kv_send, kv_recv,
    o_send, o_recv, st_send, st_recv,
):
    row_pos = lax.axis_index("row")
    col_pos = lax.axis_index("col")
    z = lax.div(row_pos, 2)
    yh = lax.rem(row_pos, 2)
    g = yh * 16 + col_pos

    def line(zz):
        return {"row": zz * 2 + yh, "col": col_pos}

    def plane(gg):
        return {"row": z * 2 + lax.div(gg, 16), "col": lax.rem(gg, 16)}

    def remote(src, dst, send, recv, device):
        return pltpu.make_async_remote_copy(
            src_ref=src, dst_ref=dst, send_sem=send, recv_sem=recv,
            device_id=device, device_id_type=pl.DeviceIdType.MESH,
        )

    def wait(ref, sem):
        pltpu.make_async_copy(ref, ref, sem).wait()

    def loop(count, body):
        lax.fori_loop(0, count, lambda i, carry: (body(i), carry)[1], 0)

    def far(i):
        return 8 + lax.div(i + 1, 2) * (1 - 2 * lax.rem(i, 2))

    def near(i):
        return lax.rem(16 + lax.div(i + 1, 2) * (1 - 2 * lax.rem(i, 2)), 16)

    loads = [
        pltpu.make_async_copy(bias_hbm, bias, local_sem.at[0]),
        pltpu.make_async_copy(wout_hbm, wout, local_sem.at[1]),
        pltpu.make_async_copy(perm_hbm, perm, local_sem.at[2]),
    ]
    barrier = pltpu.get_barrier_semaphore()

    def greet_line(i):
        pl.semaphore_signal(barrier, inc=1, device_id=line(lax.rem(z + 1 + i, 16)), device_id_type=pl.DeviceIdType.MESH)

    def greet_plane(i):
        pl.semaphore_signal(barrier, inc=1, device_id=plane(lax.rem(g + 1 + i, 32)), device_id_type=pl.DeviceIdType.MESH)

    loop(15, greet_line)
    loop(31, greet_plane)
    for load in loads:
        load.start()
    x = x_ref[...].astype(F32)
    center = x - jnp.mean(x, axis=-1, keepdims=True)
    spread = jnp.mean(center * center, axis=-1, keepdims=True)
    xs[...] = (center * lax.rsqrt(spread + 1e-05) * gain_ref[...]).astype(BF16)
    pl.semaphore_wait(barrier, 46)

    loop(15, lambda i: remote(wt_ref, wg.at[z], w_send, w_recv, line(lax.rem(z + far(i), 16))).start())
    loop(31, lambda i: remote(xs, xg.at[g], x_send, x_recv, plane(lax.rem(g + 1 + i, 32))).start())
    pltpu.make_async_copy(wt_ref, wg.at[z], w_recv).start()
    pltpu.make_async_copy(xs, xg.at[g], x_recv).start()
    wait(xg, x_recv)
    for s in range(32):
        xf[4 * s : 4 * s + 4, :] = xg[s].astype(F32)
    wait(wg, w_recv)
    for s in range(16):
        wf[6 * s : 6 * s + 6, :] = wg[s].astype(F32)
    projected = lax.dot_general(
        wf[...].astype(BF16), xf[...].astype(BF16), NT, preferred_element_type=F32
    )
    kvs[...] = projected[24:72].astype(BF16)
    qgs[0:24] = projected[0:24].astype(BF16)
    qgs[24:48] = jax.nn.sigmoid(projected[72:96]).astype(BF16)

    loop(15, lambda i: remote(kvs, kvz.at[z], kz_send, kz_recv.at[z], line(lax.rem(z + far(i), 16))).start())
    loop(31, lambda i: remote(qgs, qgb.at[g], qg_send, qg_recv, plane(lax.rem(g + 1 + i, 32))).start())
    pltpu.make_async_copy(qgs, qgb.at[g], qg_recv).start()
    pltpu.make_async_copy(kvs, kvz.at[z], kz_recv.at[z]).start()
    loads[1].wait()
    loads[2].wait()
    woutp[...] = jnp.dot(perm[...], wout[...], preferred_element_type=F32).astype(BF16)
    wait(qgb, qg_recv)

    def unpack(ref, first, dst):
        def body(s):
            dst[pl.ds(pl.multiple_of(s * 24, 8), 24), :] = ref[s, first : first + 24, :].astype(F32)

        loop(32, body)

    unpack(qgb, 0, tf)
    rows = lax.broadcasted_iota(jnp.int32, (64, 128), 0)
    lanes = lax.broadcasted_iota(jnp.int32, (64, 128), 1)
    pick = jnp.where(rows + yh * 64 == lanes, 1.0, 0.0).astype(BF16)
    qf[...] = lax.dot_general(pick, tf[...].astype(BF16), NT, preferred_element_type=F32)
    unpack(qgb, 24, tf)
    rows = lax.broadcasted_iota(jnp.int32, (8, 128), 0)
    lanes = lax.broadcasted_iota(jnp.int32, (8, 128), 1)
    pick = jnp.where((rows + yh * 64 + col_pos * 4 == lanes) & (rows < 4), 1.0, 0.0).astype(BF16)
    gate[...] = lax.dot_general(pick, tf[...].astype(BF16), NT, preferred_element_type=F32)

    def forward(i):
        s = lax.rem(z + near(i), 16)
        wait(kvz.at[s], kz_recv.at[s])
        for y in range(2):
            itself = (yh == y) & (col_pos == s)

            @pl.when(itself)
            def _():
                pltpu.make_async_copy(kvz.at[s], kvb.at[g], kv_recv).start()

            @pl.when(jnp.logical_not(itself))
            def _():
                remote(kvz.at[s], kvb.at[g], kv_send, kv_recv, {"row": z * 2 + y, "col": s}).start()

    loop(16, forward)
    loads[0].wait()
    wait(kvb, kv_recv)
    unpack(kvb, 0, tf)
    kt[...] = tf[...].astype(BF16)
    unpack(kvb, 24, tf)
    vt[...] = tf[...].astype(BF16)

    mask = heads_ref[0:16, :].astype(F32)
    rows = lax.broadcasted_iota(jnp.int32, (128, 128), 0)
    lanes = lax.broadcasted_iota(jnp.int32, (128, 128), 1)
    own = jnp.where(jnp.bitwise_and(rows, 15) == lanes, 1.0, 0.0)

    def send_parts(d):
        @pl.when(d == col_pos)
        def _():
            pltpu.make_async_copy(o_src.at[d], o_all.at[col_pos], o_recv).start()
            pltpu.make_async_copy(st_src.at[d], st_all.at[col_pos], st_recv).start()

        @pl.when(d != col_pos)
        def _():
            there = {"row": row_pos, "col": d}
            remote(o_src.at[d], o_all.at[col_pos], o_send, o_recv, there).start()
            remote(st_src.at[d], st_all.at[col_pos], st_send, st_recv, there).start()

    def attend(i):
        base = pl.multiple_of(i * 128, 128)
        queries = qf[pl.ds(pl.multiple_of(i * 8, 8), 8), :]
        spread_q = (queries[:, None, :] * mask[None]).reshape(128, 768).astype(BF16)
        scores = jnp.dot(spread_q, kt[...], preferred_element_type=F32) * (48.0**-0.5) + bias[pl.ds(base, 128), :]
        peak = jnp.max(scores, axis=-1, keepdims=True)
        expo = jnp.exp(scores - peak)
        total = jnp.sum(expo, axis=-1, keepdims=True)
        wide = lax.dot_general(expo.astype(BF16), vt[...], NT, preferred_element_type=F32)
        summed = jnp.sum(wide.reshape(8, 16, 768) * mask[None], axis=1).astype(BF16)
        peaks = jnp.sum((peak * own).reshape(8, 16, 128), axis=1)
        totals = jnp.sum((total * own).reshape(8, 16, 128), axis=1)
        for k in range(2):
            o_src[i * 2 + k] = summed[4 * k : 4 * k + 4]
            st_src[i * 2 + k, 0:4, :] = peaks[4 * k : 4 * k + 4]
            st_src[i * 2 + k, 4:8, :] = totals[4 * k : 4 * k + 4]

    loop(8, attend)
    loop(16, send_parts)
    wait(st_all, st_recv)
    stats = st_all[...]
    peak = stats[0, 0:4]
    for s in range(1, 16):
        peak = jnp.maximum(peak, stats[s, 0:4])
    factors = [jnp.exp(stats[s, 0:4] - peak) for s in range(16)]
    total = factors[0] * stats[0, 4:8]
    for s in range(1, 16):
        total = total + factors[s] * stats[s, 4:8]
    lanes = lax.broadcasted_iota(jnp.int32, (4, 128), 1)
    inverse = 1.0 / jnp.where(lanes < 16, total, 1.0)
    for s in range(16):
        fac[4 * s : 4 * s + 4, :] = jnp.where(lanes < 16, factors[s] * inverse, 0.0)
    coarse = fac[...].astype(BF16)
    fine = (fac[...] - coarse.astype(F32)).astype(BF16)
    wide = jnp.dot(coarse, heads_ref[...], preferred_element_type=F32) + jnp.dot(
        fine, heads_ref[...], preferred_element_type=F32
    )
    wait(o_all, o_recv)
    summed = wide[0:4] * o_all[0].astype(F32)
    for s in range(1, 16):
        summed = summed + wide[4 * s : 4 * s + 4] * o_all[s].astype(F32)
    attended = (summed * gate[0:4]).astype(BF16)
    out_ref[...] = jnp.dot(attended, woutp[...], preferred_element_type=F32).astype(BF16)

    wait(wg.at[pl.ds(0, 15)], w_send)
    wait(xg.at[pl.ds(0, 31)], x_send)
    wait(kvz.at[pl.ds(0, 15)], kz_send)
    wait(qgb.at[pl.ds(0, 31)], qg_send)
    wait(o_all.at[pl.ds(0, 15)], o_send)
    wait(st_all.at[pl.ds(0, 15)], st_send)
    wait(kvb.at[pl.ds(0, 31)], kv_send)


def shards(
    z_trunk, chain_id, residue, single, gain_single, w_proj, w_out, gain_trunk, w_pair, rel_table, gain_trans,
    w_up, w_down, gain_bias, w_bias,
):
    bias = pair_bias(
        z_trunk, chain_id, residue, gain_trunk, w_pair, rel_table, gain_trans, w_up, w_down, gain_bias, w_bias
    ).reshape(1024, 128)
    heads, perm = orders()
    vmem = pl.BlockSpec(memory_space=pltpu.VMEM)
    anywhere = pl.BlockSpec(memory_space=pl.ANY)
    dma = pltpu.SemaphoreType.DMA
    return pl.pallas_call(
        main_kernel,
        out_shape=jax.ShapeDtypeStruct((4, 768), BF16),
        in_specs=[vmem] * 4 + [anywhere] * 3,
        out_specs=vmem,
        scratch_shapes=[
            pltpu.VMEM((4, 768), BF16),
            pltpu.VMEM((32, 4, 768), BF16),
            pltpu.VMEM((16, 6, 768), BF16),
            pltpu.VMEM((128, 768), F32),
            pltpu.VMEM((96, 768), F32),
            pltpu.VMEM((48, 128), BF16),
            pltpu.VMEM((48, 128), BF16),
            pltpu.VMEM((16, 48, 128), BF16),
            pltpu.VMEM((32, 48, 128), BF16),
            pltpu.VMEM((32, 48, 128), BF16),
            pltpu.VMEM((768, 128), F32),
            pltpu.VMEM((768, 128), BF16),
            pltpu.VMEM((768, 128), BF16),
            pltpu.VMEM((64, 768), F32),
            pltpu.VMEM((8, 768), F32),
            pltpu.VMEM((1024, 128), F32),
            pltpu.VMEM((768, 768), BF16),
            pltpu.VMEM((768, 768), BF16),
            pltpu.VMEM((768, 768), BF16),
            pltpu.VMEM((16, 4, 768), BF16),
            pltpu.VMEM((16, 4, 768), BF16),
            pltpu.VMEM((16, 8, 128), F32),
            pltpu.VMEM((16, 8, 128), F32),
            pltpu.VMEM((64, 128), F32),
            dma((3,)),
            dma, dma, dma, dma, dma, dma, dma, dma((16,)), dma, dma, dma, dma, dma, dma,
        ],
        compiler_params=pltpu.CompilerParams(
            collective_id=0, has_side_effects=True, vmem_limit_bytes=40 << 20
        ),
    )(
        single, gain_single.reshape(1, 768), w_proj.T, jnp.asarray(heads, BF16), bias, w_out,
        jnp.asarray(perm, BF16),
    )


def solution(mesh):
    return jax.shard_map(
        shards,
        mesh=mesh,
        in_specs=(
            P("row", "col", None), P(), P(), P(("row", "col"), None), P(), P(None, ("row", "col")),
            P(), P(), P(), P(), P(), P(), P(), P(), P(),
        ),
        out_specs=P(("row", "col"), None),
        check_vma=False,
    )
```

```python
import functools

import jax
import jax.numpy as jnp
import numpy as np
from jax import lax
from jax.experimental import pallas as pl
from jax.experimental.pallas import tpu as pltpu
from jax.sharding import PartitionSpec as P

NT = (((1,), (1,)), ((), ()))
F32 = jnp.float32
BF16 = jnp.bfloat16
BIG = 1 << 20
QB = 16
B0, B1, B2 = 1, 2, 1


def norm_cols(values):
    center = values - jnp.mean(values, axis=0, keepdims=True)
    spread = jnp.mean(center * center, axis=0, keepdims=True)
    return (center * lax.rsqrt(spread + 1e-05)).astype(BF16)


def interval_bounds(chain_k, res_k):
    bins = lax.broadcasted_iota(jnp.int32, (128, 128), 0)
    base = jnp.broadcast_to(chain_k * 64, (128, 128))
    res = jnp.broadcast_to(res_k, (128, 128))
    shifted = res + bins - 32
    inside = (shifted >= 0) & (shifted <= 63)
    low = jnp.where(inside, base + shifted, BIG)
    high = jnp.where(inside, base + shifted, -BIG)

    def put(low, high, index, new_low, new_high):
        hit = bins == index
        return jnp.where(hit, new_low, low), jnp.where(hit, new_high, high)

    low, high = put(low, high, 0, base, base + res - 32)
    low, high = put(low, high, 64, base + res + 32, base + 63)
    low, high = put(low, high, 65, jnp.full_like(base, -BIG), base - 1)
    low, high = put(low, high, 66, base, base + 63)
    low, high = put(low, high, 67, base + 64, base + 127)
    low, high = put(low, high, 68, base + 128, jnp.full_like(base, BIG))
    low, high = put(low, high, 69, jnp.full_like(base, -BIG), base - 65)
    low, high = put(low, high, 70, base + 64, jnp.full_like(base, BIG))
    unused = bins > 70
    return jnp.where(unused, BIG, low), jnp.where(unused, -BIG, high)


def prepare_bias(chain_k, res_k, refs, scratch):
    gtrunk_ref, wpair_ref, rel_ref, gtrans_ref, wup_ref, wdown_ref, gbias_ref, wbias_ref = refs
    low_ref, high_ref, wcat, wup, wdn, wb, rel = scratch
    low, high = interval_bounds(chain_k, res_k)
    low_ref[...] = low
    high_ref[...] = high
    wcat[:, :128] = (wpair_ref[...].astype(F32).T * gtrunk_ref[...]).astype(BF16)
    rel[...] = jnp.zeros_like(rel)
    rel[0:69, :] = rel_ref[0:69, :].astype(F32)
    rel[69:70, :] = rel_ref[64:65, :].astype(F32)
    rel[70:71, :] = rel_ref[65:66, :].astype(F32)
    wcat[:, 128:] = rel[...].T.astype(BF16)
    for t in range(2):
        up = wup_ref[t].astype(F32).T * gtrans_ref[t : t + 1, :]
        wup[t, :256] = (up[:256] * 0.5).astype(BF16)
        wup[t, 256:] = up[256:].astype(BF16)
        wdn[t] = wdown_ref[t].astype(F32).T.astype(BF16)
    wb[...] = (wbias_ref[...].astype(F32) * gbias_ref[...]).astype(BF16)


def bias_block(first, codes, z_ref, scratch, bias):
    low_ref, high_ref, wcat, wup, wdn, wb, _ = scratch
    low = low_ref[...]
    high = high_ref[...]
    tiles = [z_ref[first + j].astype(F32).T for j in range(QB)]
    normed = norm_cols(jnp.concatenate(tiles, axis=1))
    hots = []
    for j in range(QB):
        code = codes(first + j)
        hots.append(jnp.where((low <= code) & (high >= code), 1.0, 0.0).astype(BF16))
    both = jnp.concatenate([normed, jnp.concatenate(hots, axis=1)], axis=0)
    pair = jnp.dot(wcat[...], both, preferred_element_type=F32)
    for t in range(2):
        expanded = jnp.dot(wup[t], norm_cols(pair), preferred_element_type=F32)
        half = expanded[:256]
        product = half * expanded[256:]
        swiglu = (product + product * jnp.tanh(half)).astype(BF16)
        pair = pair + jnp.dot(wdn[t], swiglu, preferred_element_type=F32)
    out = jnp.dot(wb[...], norm_cols(pair), preferred_element_type=F32)
    for j in range(QB):
        bias[pl.ds(pl.multiple_of((first + j) * 16, 16), 16), :] = out[:, j * 128 : (j + 1) * 128]


def orders():
    natural = np.zeros(768, np.int64)
    for g in range(32):
        for zk in range(4):
            for i in range(6):
                natural[g * 24 + zk * 6 + i] = 192 * zk + 6 * g + i
    heads = np.zeros((128, 768), np.float32)
    heads[natural // 48, np.arange(768)] = 1.0
    perm = np.zeros((768, 768), np.float32)
    perm[np.arange(768), natural] = 1.0
    return heads, perm


def main_kernel(
    chain_sm, res_sm, x_ref, gain_ref, wt_ref, heads_ref, chain_ref, res_ref,
    gtrunk_ref, wpair_ref, rel_ref, gtrans_ref, wup_ref, wdown_ref, gbias_ref, wbias_ref,
    z_hbm, wout_hbm, perm_hbm, out_ref,
    xs, xg, wg, xf, wf, kvs, qgs, kvz, kvb, qgb, tf, kt, vt, qf, gate, bias, wout, perm, woutp,
    o_src, o_all, st_src, st_all, fac, zs, low, high, wcat, wup, wdn, wb, rel,
    local_sem, w_send, w_recv, x_send, x_recv, qg_send, qg_recv, kz_send, kz_recv, kv_send, kv_recv,
    o_send, o_recv, st_send, st_recv,
):
    row_pos = lax.axis_index("row")
    col_pos = lax.axis_index("col")
    z = lax.div(row_pos, 2)
    yh = lax.rem(row_pos, 2)
    g = yh * 16 + col_pos

    def line(zz):
        return {"row": zz * 2 + yh, "col": col_pos}

    def plane(gg):
        return {"row": z * 2 + lax.div(gg, 16), "col": lax.rem(gg, 16)}

    def remote(src, dst, send, recv, device):
        return pltpu.make_async_remote_copy(
            src_ref=src, dst_ref=dst, send_sem=send, recv_sem=recv,
            device_id=device, device_id_type=pl.DeviceIdType.MESH,
        )

    def wait(ref, sem):
        pltpu.make_async_copy(ref, ref, sem).wait()

    def loop(count, body):
        lax.fori_loop(0, count, lambda i, carry: (body(i), carry)[1], 0)

    def far(i):
        return 8 + lax.div(i + 1, 2) * (1 - 2 * lax.rem(i, 2))

    def near(i):
        return lax.rem(16 + lax.div(i + 1, 2) * (1 - 2 * lax.rem(i, 2)), 16)


    loads = [
        pltpu.make_async_copy(z_hbm, zs, local_sem.at[0]),
        pltpu.make_async_copy(wout_hbm, wout, local_sem.at[1]),
        pltpu.make_async_copy(perm_hbm, perm, local_sem.at[2]),
    ]
    barrier = pltpu.get_barrier_semaphore()

    def greet_line(i):
        pl.semaphore_signal(barrier, inc=1, device_id=line(lax.rem(z + 1 + i, 16)), device_id_type=pl.DeviceIdType.MESH)

    def greet_plane(i):
        pl.semaphore_signal(barrier, inc=1, device_id=plane(lax.rem(g + 1 + i, 32)), device_id_type=pl.DeviceIdType.MESH)

    loop(15, greet_line)
    loop(31, greet_plane)
    for load in loads:
        load.start()
    x = x_ref[...].astype(F32)
    center = x - jnp.mean(x, axis=-1, keepdims=True)
    spread = jnp.mean(center * center, axis=-1, keepdims=True)
    xs[...] = (center * lax.rsqrt(spread + 1e-05) * gain_ref[...]).astype(BF16)
    pair_scratch = (low, high, wcat, wup, wdn, wb, rel)
    prepare_bias(
        chain_ref[pl.ds(col_pos, 1), :], res_ref[pl.ds(col_pos, 1), :],
        (gtrunk_ref, wpair_ref, rel_ref, gtrans_ref, wup_ref, wdown_ref, gbias_ref, wbias_ref), pair_scratch,
    )

    def code_of(index):
        token = row_pos * 64 + index
        return chain_sm[token] * 64 + res_sm[token]

    def blocks(start, count):
        loop(count, lambda i: bias_block((start + i) * QB, code_of, zs, pair_scratch, bias))

    loads[0].wait()
    blocks(0, B0)
    pl.semaphore_wait(barrier, 46)

    loop(15, lambda i: remote(wt_ref, wg.at[z], w_send, w_recv, line(lax.rem(z + far(i), 16))).start())
    loop(31, lambda i: remote(xs, xg.at[g], x_send, x_recv, plane(lax.rem(g + 1 + i, 32))).start())
    pltpu.make_async_copy(wt_ref, wg.at[z], w_recv).start()
    pltpu.make_async_copy(xs, xg.at[g], x_recv).start()
    blocks(B0, B1)
    wait(xg, x_recv)
    for s in range(32):
        xf[4 * s : 4 * s + 4, :] = xg[s].astype(F32)
    wait(wg, w_recv)
    for s in range(16):
        wf[6 * s : 6 * s + 6, :] = wg[s].astype(F32)
    projected = lax.dot_general(
        wf[...].astype(BF16), xf[...].astype(BF16), NT, preferred_element_type=F32
    )
    kvs[...] = projected[24:72].astype(BF16)
    qgs[0:24] = projected[0:24].astype(BF16)
    qgs[24:48] = jax.nn.sigmoid(projected[72:96]).astype(BF16)

    loop(15, lambda i: remote(kvs, kvz.at[z], kz_send, kz_recv.at[z], line(lax.rem(z + far(i), 16))).start())
    loop(31, lambda i: remote(qgs, qgb.at[g], qg_send, qg_recv, plane(lax.rem(g + 1 + i, 32))).start())
    pltpu.make_async_copy(qgs, qgb.at[g], qg_recv).start()
    pltpu.make_async_copy(kvs, kvz.at[z], kz_recv.at[z]).start()
    loads[1].wait()
    loads[2].wait()
    blocks(B0 + B1, B2)
    woutp[...] = jnp.dot(perm[...], wout[...], preferred_element_type=F32).astype(BF16)
    wait(qgb, qg_recv)

    def unpack(ref, first, dst):
        def body(s):
            dst[pl.ds(pl.multiple_of(s * 24, 8), 24), :] = ref[s, first : first + 24, :].astype(F32)

        loop(32, body)

    unpack(qgb, 0, tf)
    rows = lax.broadcasted_iota(jnp.int32, (64, 128), 0)
    lanes = lax.broadcasted_iota(jnp.int32, (64, 128), 1)
    pick = jnp.where(rows + yh * 64 == lanes, 1.0, 0.0).astype(BF16)
    qf[...] = lax.dot_general(pick, tf[...].astype(BF16), NT, preferred_element_type=F32)
    unpack(qgb, 24, tf)
    rows = lax.broadcasted_iota(jnp.int32, (8, 128), 0)
    lanes = lax.broadcasted_iota(jnp.int32, (8, 128), 1)
    pick = jnp.where((rows + yh * 64 + col_pos * 4 == lanes) & (rows < 4), 1.0, 0.0).astype(BF16)
    gate[...] = lax.dot_general(pick, tf[...].astype(BF16), NT, preferred_element_type=F32)


    def forward(i):
        s = lax.rem(z + near(i), 16)
        wait(kvz.at[s], kz_recv.at[s])
        for y in range(2):
            itself = (yh == y) & (col_pos == s)

            @pl.when(itself)
            def _():
                pltpu.make_async_copy(kvz.at[s], kvb.at[g], kv_recv).start()

            @pl.when(jnp.logical_not(itself))
            def _():
                remote(kvz.at[s], kvb.at[g], kv_send, kv_recv, {"row": z * 2 + y, "col": s}).start()

    loop(16, forward)
    blocks(B0 + B1 + B2, 64 // QB - B0 - B1 - B2)
    wait(kvb, kv_recv)
    unpack(kvb, 0, tf)
    kt[...] = tf[...].astype(BF16)
    unpack(kvb, 24, tf)
    vt[...] = tf[...].astype(BF16)

    mask = heads_ref[0:16, :].astype(F32)
    rows = lax.broadcasted_iota(jnp.int32, (128, 128), 0)
    lanes = lax.broadcasted_iota(jnp.int32, (128, 128), 1)
    own = jnp.where(jnp.bitwise_and(rows, 15) == lanes, 1.0, 0.0)

    def send_parts(d):
        @pl.when(d == col_pos)
        def _():
            pltpu.make_async_copy(o_src.at[d], o_all.at[col_pos], o_recv).start()
            pltpu.make_async_copy(st_src.at[d], st_all.at[col_pos], st_recv).start()

        @pl.when(d != col_pos)
        def _():
            there = {"row": row_pos, "col": d}
            remote(o_src.at[d], o_all.at[col_pos], o_send, o_recv, there).start()
            remote(st_src.at[d], st_all.at[col_pos], st_send, st_recv, there).start()

    def attend(i):
        base = pl.multiple_of(i * 128, 128)
        queries = qf[pl.ds(pl.multiple_of(i * 8, 8), 8), :]
        spread_q = (queries[:, None, :] * mask[None]).reshape(128, 768).astype(BF16)
        scores = jnp.dot(spread_q, kt[...], preferred_element_type=F32) * (48.0**-0.5) + bias[pl.ds(base, 128), :]
        peak = jnp.max(scores, axis=-1, keepdims=True)
        expo = jnp.exp(scores - peak)
        total = jnp.sum(expo, axis=-1, keepdims=True)
        wide = lax.dot_general(expo.astype(BF16), vt[...], NT, preferred_element_type=F32)
        summed = jnp.sum(wide.reshape(8, 16, 768) * mask[None], axis=1).astype(BF16)
        peaks = jnp.sum((peak * own).reshape(8, 16, 128), axis=1)
        totals = jnp.sum((total * own).reshape(8, 16, 128), axis=1)
        for k in range(2):
            o_src[i * 2 + k] = summed[4 * k : 4 * k + 4]
            st_src[i * 2 + k, 0:4, :] = peaks[4 * k : 4 * k + 4]
            st_src[i * 2 + k, 4:8, :] = totals[4 * k : 4 * k + 4]

    loop(8, attend)
    loop(16, send_parts)
    wait(st_all, st_recv)
    stats = st_all[...]
    peak = stats[0, 0:4]
    for s in range(1, 16):
        peak = jnp.maximum(peak, stats[s, 0:4])
    factors = [jnp.exp(stats[s, 0:4] - peak) for s in range(16)]
    total = factors[0] * stats[0, 4:8]
    for s in range(1, 16):
        total = total + factors[s] * stats[s, 4:8]
    lanes = lax.broadcasted_iota(jnp.int32, (4, 128), 1)
    inverse = 1.0 / jnp.where(lanes < 16, total, 1.0)
    for s in range(16):
        fac[4 * s : 4 * s + 4, :] = jnp.where(lanes < 16, factors[s] * inverse, 0.0)
    coarse = fac[...].astype(BF16)
    fine = (fac[...] - coarse.astype(F32)).astype(BF16)
    wide = jnp.dot(coarse, heads_ref[...], preferred_element_type=F32) + jnp.dot(
        fine, heads_ref[...], preferred_element_type=F32
    )
    wait(o_all, o_recv)
    summed = wide[0:4] * o_all[0].astype(F32)
    for s in range(1, 16):
        summed = summed + wide[4 * s : 4 * s + 4] * o_all[s].astype(F32)
    attended = (summed * gate[0:4]).astype(BF16)
    out_ref[...] = jnp.dot(attended, woutp[...], preferred_element_type=F32).astype(BF16)

    wait(wg.at[pl.ds(0, 15)], w_send)
    wait(xg.at[pl.ds(0, 31)], x_send)
    wait(kvz.at[pl.ds(0, 15)], kz_send)
    wait(qgb.at[pl.ds(0, 31)], qg_send)
    wait(o_all.at[pl.ds(0, 15)], o_send)
    wait(st_all.at[pl.ds(0, 15)], st_send)
    wait(kvb.at[pl.ds(0, 31)], kv_send)


def shards(
    z_trunk, chain_id, residue, single, gain_single, w_proj, w_out, gain_trunk, w_pair, rel_table, gain_trans,
    w_up, w_down, gain_bias, w_bias,
):
    heads, perm = orders()
    vmem = pl.BlockSpec(memory_space=pltpu.VMEM)
    anywhere = pl.BlockSpec(memory_space=pl.ANY)
    dma = pltpu.SemaphoreType.DMA
    return pl.pallas_call(
        main_kernel,
        out_shape=jax.ShapeDtypeStruct((4, 768), BF16),
        in_specs=[pl.BlockSpec(memory_space=pltpu.SMEM)] * 2 + [vmem] * 14 + [anywhere] * 3,
        out_specs=vmem,
        scratch_shapes=[
            pltpu.VMEM((4, 768), BF16),
            pltpu.VMEM((32, 4, 768), BF16),
            pltpu.VMEM((16, 6, 768), BF16),
            pltpu.VMEM((128, 768), F32),
            pltpu.VMEM((96, 768), F32),
            pltpu.VMEM((48, 128), BF16),
            pltpu.VMEM((48, 128), BF16),
            pltpu.VMEM((16, 48, 128), BF16),
            pltpu.VMEM((32, 48, 128), BF16),
            pltpu.VMEM((32, 48, 128), BF16),
            pltpu.VMEM((768, 128), F32),
            pltpu.VMEM((768, 128), BF16),
            pltpu.VMEM((768, 128), BF16),
            pltpu.VMEM((64, 768), F32),
            pltpu.VMEM((8, 768), F32),
            pltpu.VMEM((1024, 128), F32),
            pltpu.VMEM((768, 768), BF16),
            pltpu.VMEM((768, 768), BF16),
            pltpu.VMEM((768, 768), BF16),
            pltpu.VMEM((16, 4, 768), BF16),
            pltpu.VMEM((16, 4, 768), BF16),
            pltpu.VMEM((16, 8, 128), F32),
            pltpu.VMEM((16, 8, 128), F32),
            pltpu.VMEM((64, 128), F32),
            pltpu.VMEM((64, 128, 128), BF16),
            pltpu.VMEM((128, 128), jnp.int32),
            pltpu.VMEM((128, 128), jnp.int32),
            pltpu.VMEM((128, 256), BF16),
            pltpu.VMEM((2, 512, 128), BF16),
            pltpu.VMEM((2, 128, 256), BF16),
            pltpu.VMEM((16, 128), BF16),
            pltpu.VMEM((128, 128), F32),
            dma((3,)),
            dma, dma, dma, dma, dma, dma, dma, dma((16,)), dma, dma, dma, dma, dma, dma,
        ],
        compiler_params=pltpu.CompilerParams(
            collective_id=0, has_side_effects=True, vmem_limit_bytes=40 << 20
        ),
    )(
        chain_id, residue, single, gain_single.reshape(1, 768), w_proj.T, jnp.asarray(heads, BF16),
        chain_id.reshape(16, 128), residue.reshape(16, 128), gain_trunk.reshape(1, 128), w_pair, rel_table, gain_trans,
        w_up, w_down, gain_bias.reshape(1, 128), w_bias.T, z_trunk, w_out, jnp.asarray(perm, BF16),
    )


def solution(mesh):
    return jax.shard_map(
        shards,
        mesh=mesh,
        in_specs=(
            P("row", "col", None), P(), P(), P(("row", "col"), None), P(), P(None, ("row", "col")),
            P(), P(), P(), P(), P(), P(), P(), P(), P(),
        ),
        out_specs=P(("row", "col"), None),
        check_vma=False,
    )
```

```python
import functools

import jax
import jax.numpy as jnp
import numpy as np
from jax import lax
from jax.experimental import pallas as pl
from jax.experimental.pallas import tpu as pltpu
from jax.sharding import PartitionSpec as P

NT = (((1,), (1,)), ((), ()))
F32 = jnp.float32
BF16 = jnp.bfloat16
BIG = 1 << 20
QB = 16
B0, B1, B2 = 1, 2, 1
QA = 16
OFFSETS = (2, 1, 3, 0)


def norm_cols(values):
    center = values - jnp.mean(values, axis=0, keepdims=True)
    spread = jnp.mean(center * center, axis=0, keepdims=True)
    return (center * lax.rsqrt(spread + 1e-05)).astype(BF16)


def interval_bounds(chain_k, res_k):
    bins = lax.broadcasted_iota(jnp.int32, (128, 128), 0)
    base = jnp.broadcast_to(chain_k * 64, (128, 128))
    res = jnp.broadcast_to(res_k, (128, 128))
    shifted = res + bins - 32
    inside = (shifted >= 0) & (shifted <= 63)
    low = jnp.where(inside, base + shifted, BIG)
    high = jnp.where(inside, base + shifted, -BIG)

    def put(low, high, index, new_low, new_high):
        hit = bins == index
        return jnp.where(hit, new_low, low), jnp.where(hit, new_high, high)

    low, high = put(low, high, 0, base, base + res - 32)
    low, high = put(low, high, 64, base + res + 32, base + 63)
    low, high = put(low, high, 65, jnp.full_like(base, -BIG), base - 1)
    low, high = put(low, high, 66, base, base + 63)
    low, high = put(low, high, 67, base + 64, base + 127)
    low, high = put(low, high, 68, base + 128, jnp.full_like(base, BIG))
    low, high = put(low, high, 69, jnp.full_like(base, -BIG), base - 65)
    low, high = put(low, high, 70, base + 64, jnp.full_like(base, BIG))
    unused = bins > 70
    return jnp.where(unused, BIG, low), jnp.where(unused, -BIG, high)


def prepare_bias(chain_k, res_k, refs, scratch):
    gtrunk_ref, wpair_ref, rel_ref, gtrans_ref, wup_ref, wdown_ref, gbias_ref, wbias_ref = refs
    low_ref, high_ref, wcat, wup, wdn, wb, rel = scratch
    low, high = interval_bounds(chain_k, res_k)
    low_ref[...] = low
    high_ref[...] = high
    wcat[:, :128] = (wpair_ref[...].astype(F32).T * gtrunk_ref[...]).astype(BF16)
    rel[...] = jnp.zeros_like(rel)
    rel[0:69, :] = rel_ref[0:69, :].astype(F32)
    rel[69:70, :] = rel_ref[64:65, :].astype(F32)
    rel[70:71, :] = rel_ref[65:66, :].astype(F32)
    wcat[:, 128:] = rel[...].T.astype(BF16)
    for t in range(2):
        up = wup_ref[t].astype(F32).T * gtrans_ref[t : t + 1, :]
        wup[t, :256] = (up[:256] * 0.5).astype(BF16)
        wup[t, 256:] = up[256:].astype(BF16)
        wdn[t] = wdown_ref[t].astype(F32).T.astype(BF16)
    wb[...] = (wbias_ref[...].astype(F32) * gbias_ref[...]).astype(BF16)


def bias_block(first, codes, z_ref, scratch, bias):
    low_ref, high_ref, wcat, wup, wdn, wb, _ = scratch
    low = low_ref[...]
    high = high_ref[...]
    tiles = [z_ref[first + j].astype(F32).T for j in range(QB)]
    normed = norm_cols(jnp.concatenate(tiles, axis=1))
    hots = []
    for j in range(QB):
        code = codes(first + j)
        hots.append(jnp.where((low <= code) & (high >= code), 1.0, 0.0).astype(BF16))
    both = jnp.concatenate([normed, jnp.concatenate(hots, axis=1)], axis=0)
    pair = jnp.dot(wcat[...], both, preferred_element_type=F32)
    for t in range(2):
        expanded = jnp.dot(wup[t], norm_cols(pair), preferred_element_type=F32)
        half = expanded[:256]
        product = half * expanded[256:]
        swiglu = (product + product * jnp.tanh(half)).astype(BF16)
        pair = pair + jnp.dot(wdn[t], swiglu, preferred_element_type=F32)
    out = jnp.dot(wb[...], norm_cols(pair), preferred_element_type=F32)
    for j in range(QB):
        bias[pl.ds(pl.multiple_of((first + j) * 16, 16), 16), :] = out[:, j * 128 : (j + 1) * 128]


def orders():
    natural = np.zeros(768, np.int64)
    for g in range(32):
        for zk in range(4):
            for i in range(6):
                natural[g * 24 + zk * 6 + i] = 192 * zk + 6 * g + i
    heads = np.zeros((128, 768), np.float32)
    heads[natural // 48, np.arange(768)] = 1.0
    perm = np.zeros((768, 768), np.float32)
    perm[np.arange(768), natural] = 1.0
    return heads, perm


HBM_ARGS = (
    "x", "gain", "wt", "chain_sm", "res_sm", "chain", "res", "gtrunk", "wpair", "rel", "gtrans", "wup", "wdown", "gbias",
    "wbias", "z", "heads", "wout", "perm",
)


def main_kernel(*refs):
    count = len(HBM_ARGS)
    source = dict(zip(HBM_ARGS, refs[:count]))
    out_ref = refs[count]
    held = dict(zip(HBM_ARGS, refs[count + 1 : 2 * count + 1]))
    (
        xs, xg, wg, xf, wf, kvs, qgs, kvz, kvb, qgb, kt, vt, qf, spread, gate, bias, woutp,
        o_src, o_all, st_src, st_all, fac, low, high, wcat, wup, wdn, wb, rel,
        local_sem, w_send, w_recv, x_send, x_recv, qg_send, qg_recv, kz_send, kz_recv, kv_send, kv_recv,
        o_send, o_recv, st_send, st_recv,
    ) = refs[2 * count + 1 :]
    row_pos = lax.axis_index("row")
    col_pos = lax.axis_index("col")
    z = lax.div(row_pos, 2)
    yh = lax.rem(row_pos, 2)
    g = yh * 16 + col_pos
    middle = lax.rem(lax.div(z + 4, 8), 2)

    def line(zz):
        return {"row": zz * 2 + yh, "col": col_pos}

    def plane(gg):
        return {"row": z * 2 + lax.div(gg, 16), "col": lax.rem(gg, 16)}

    def remote(src, dst, send, recv, device):
        return pltpu.make_async_remote_copy(
            src_ref=src, dst_ref=dst, send_sem=send, recv_sem=recv,
            device_id=device, device_id_type=pl.DeviceIdType.MESH,
        )

    def wait(ref, sem):
        pltpu.make_async_copy(ref, ref, sem).wait()

    def loop(count, body):
        lax.fori_loop(0, count, lambda i, carry: (body(i), carry)[1], 0)

    def far(i):
        return 8 + lax.div(i + 1, 2) * (1 - 2 * lax.rem(i, 2))

    def near(i):
        return lax.rem(16 + lax.div(i + 1, 2) * (1 - 2 * lax.rem(i, 2)), 16)


    loads = {
        name: pltpu.make_async_copy(source[name], held[name], local_sem.at[index])
        for index, name in enumerate(HBM_ARGS)
    }
    barrier = pltpu.get_barrier_semaphore()

    def greet_line(i):
        pl.semaphore_signal(barrier, inc=1, device_id=line(lax.rem(z + 1 + i, 16)), device_id_type=pl.DeviceIdType.MESH)

    def greet_plane(i):
        pl.semaphore_signal(barrier, inc=1, device_id=plane(lax.rem(g + 1 + i, 32)), device_id_type=pl.DeviceIdType.MESH)

    loop(15, greet_line)
    loop(31, greet_plane)
    for name in HBM_ARGS:
        loads[name].start()
    loads["x"].wait()
    loads["gain"].wait()
    x = held["x"][...].astype(F32)
    center = x - jnp.mean(x, axis=-1, keepdims=True)
    deviation = jnp.mean(center * center, axis=-1, keepdims=True)
    gain = jnp.concatenate([held["gain"][k : k + 1, :] for k in range(6)], axis=1)
    xs[...] = (center * lax.rsqrt(deviation + 1e-05) * gain).astype(BF16)
    pair_args = ("gtrunk", "wpair", "rel", "gtrans", "wup", "wdown", "gbias", "wbias")
    for name in ("wt", "heads", "chain", "res", "chain_sm", "res_sm", "z") + pair_args:
        loads[name].wait()
    pair_scratch = (low, high, wcat, wup, wdn, wb, rel)
    prepare_bias(
        held["chain"][pl.ds(col_pos, 1), :], held["res"][pl.ds(col_pos, 1), :],
        [held[name] for name in pair_args], pair_scratch,
    )

    def code_of(index):
        token = row_pos * 64 + index
        return held["chain_sm"][token] * 64 + held["res_sm"][token]

    def blocks(start, count):
        loop(count, lambda i: bias_block((start + i) * QB, code_of, held["z"], pair_scratch, bias))

    blocks(0, B0)
    pl.semaphore_wait(barrier, 46)

    wt = held["wt"]
    loop(15, lambda i: remote(wt, wg.at[z], w_send, w_recv.at[middle], line(lax.rem(z + far(i), 16))).start())
    loop(31, lambda i: remote(xs, xg.at[g], x_send, x_recv, plane(lax.rem(g + 1 + i, 32))).start())
    pltpu.make_async_copy(wt, wg.at[z], w_recv.at[middle]).start()
    pltpu.make_async_copy(xs, xg.at[g], x_recv).start()
    blocks(B0, B1)
    wait(xg, x_recv)
    for s in range(32):
        xf[4 * s : 4 * s + 4, :] = xg[s].astype(F32)
    tokens = xf[...].astype(BF16)
    wait(wg.at[pl.ds(4, 8)], w_recv.at[1])
    for s in range(8):
        wf[6 * s : 6 * s + 6, :] = wg[4 + s].astype(F32)
    kvs[...] = lax.dot_general(wf[...].astype(BF16), tokens, NT, preferred_element_type=F32).astype(BF16)

    loop(15, lambda i: remote(kvs, kvz.at[z], kz_send, kz_recv.at[z], line(lax.rem(z + far(i), 16))).start())
    pltpu.make_async_copy(kvs, kvz.at[z], kz_recv.at[z]).start()
    loads["wout"].wait()
    loads["perm"].wait()
    woutp[...] = jnp.dot(held["perm"][...], held["wout"][...], preferred_element_type=F32).astype(BF16)
    wait(wg.at[pl.ds(0, 8)], w_recv.at[0])
    for s in range(8):
        wf[6 * s : 6 * s + 6, :] = wg[s if s < 4 else s + 8].astype(F32)
    projected = lax.dot_general(
        wf[...].astype(BF16), xf[...].astype(BF16), NT, preferred_element_type=F32
    )
    qgs[0:24] = projected[0:24].astype(BF16)
    qgs[24:48] = jax.nn.sigmoid(projected[24:48]).astype(BF16)
    loop(31, lambda i: remote(qgs, qgb.at[g], qg_send, qg_recv, plane(lax.rem(g + 1 + i, 32))).start())
    pltpu.make_async_copy(qgs, qgb.at[g], qg_recv).start()
    blocks(B0 + B1, B2)
    wait(qgb, qg_recv)

    def unpack(ref, first):
        return ref[:, first : first + 24, :].astype(F32).reshape(768, 128).astype(BF16)

    rows = lax.broadcasted_iota(jnp.int32, (64, 128), 0)
    lanes = lax.broadcasted_iota(jnp.int32, (64, 128), 1)
    pick = jnp.where(rows + yh * 64 == lanes, 1.0, 0.0).astype(BF16)
    qf[...] = lax.dot_general(pick, unpack(qgb, 0), NT, preferred_element_type=F32)
    mask = held["heads"][0:16, :].astype(F32)

    def spread_queries(i):
        queries = qf[pl.ds(pl.multiple_of(i * 8, 8), 8), :]
        spread[pl.ds(pl.multiple_of(i * 128, 128), 128), :] = (
            (queries[:, None, :] * mask[None]).reshape(128, 768).astype(BF16)
        )

    loop(8, spread_queries)
    rows = lax.broadcasted_iota(jnp.int32, (8, 128), 0)
    lanes = lax.broadcasted_iota(jnp.int32, (8, 128), 1)
    pick = jnp.where((rows + yh * 64 + col_pos * 4 == lanes) & (rows < 4), 1.0, 0.0).astype(BF16)
    gate[...] = lax.dot_general(pick, unpack(qgb, 24), NT, preferred_element_type=F32)


    def forward(i):
        s = lax.rem(z + near(i), 16)
        wait(kvz.at[s], kz_recv.at[s])
        for y in range(2):
            itself = (yh == y) & (col_pos == s)

            @pl.when(itself)
            def _():
                pltpu.make_async_copy(kvz.at[s], kvb.at[g], kv_recv).start()

            @pl.when(jnp.logical_not(itself))
            def _():
                remote(kvz.at[s], kvb.at[g], kv_send, kv_recv, {"row": z * 2 + y, "col": s}).start()

    loop(16, forward)
    blocks(B0 + B1 + B2, 64 // QB - B0 - B1 - B2)
    wait(kvb, kv_recv)
    kt[...] = unpack(kvb, 0)
    vt[...] = unpack(kvb, 24)
    rows = lax.broadcasted_iota(jnp.int32, (QA * 16, 128), 0)
    lanes = lax.broadcasted_iota(jnp.int32, (QA * 16, 128), 1)
    own = jnp.where(jnp.bitwise_and(rows, 15) == lanes, 1.0, 0.0)

    def send_parts(d):
        @pl.when(d == col_pos)
        def _():
            pltpu.make_async_copy(o_src.at[d], o_all.at[col_pos], o_recv).start()
            pltpu.make_async_copy(st_src.at[d], st_all.at[col_pos], st_recv).start()

        @pl.when(d != col_pos)
        def _():
            there = {"row": row_pos, "col": d}
            remote(o_src.at[d], o_all.at[col_pos], o_send, o_recv, there).start()
            remote(st_src.at[d], st_all.at[col_pos], st_send, st_recv, there).start()

    def attend(i):
        base = pl.multiple_of(i * (QA * 16), QA * 16)
        scores = jnp.dot(spread[pl.ds(base, QA * 16), :], kt[...], preferred_element_type=F32)
        scores = scores * (48.0**-0.5) + bias[pl.ds(base, QA * 16), :]
        peak = jnp.max(scores, axis=-1, keepdims=True)
        expo = jnp.exp(scores - peak)
        total = jnp.sum(expo, axis=-1, keepdims=True)
        wide = lax.dot_general(expo.astype(BF16), vt[...], NT, preferred_element_type=F32)
        summed = jnp.sum(wide.reshape(QA, 16, 768) * mask[None], axis=1).astype(BF16)
        peaks = jnp.sum((peak * own).reshape(QA, 16, 128), axis=1)
        totals = jnp.sum((total * own).reshape(QA, 16, 128), axis=1)
        for k in range(QA // 4):
            part = i * (QA // 4) + k
            o_src[part] = summed[4 * k : 4 * k + 4]
            st_src[part, 0:4, :] = peaks[4 * k : 4 * k + 4]
            st_src[part, 4:8, :] = totals[4 * k : 4 * k + 4]

    parts = 64 // QA
    first = lax.div(col_pos, QA // 4)
    for offset in OFFSETS:
        block = lax.rem(first + offset, parts)
        attend(block)
        loop(QA // 4, lambda k, block=block: send_parts(block * (QA // 4) + k))
    wait(st_all, st_recv)
    stats = st_all[...]
    peak = stats[0, 0:4]
    for s in range(1, 16):
        peak = jnp.maximum(peak, stats[s, 0:4])
    factors = [jnp.exp(stats[s, 0:4] - peak) for s in range(16)]
    total = factors[0] * stats[0, 4:8]
    for s in range(1, 16):
        total = total + factors[s] * stats[s, 4:8]
    lanes = lax.broadcasted_iota(jnp.int32, (4, 128), 1)
    inverse = 1.0 / jnp.where(lanes < 16, total, 1.0)
    for s in range(16):
        fac[4 * s : 4 * s + 4, :] = jnp.where(lanes < 16, factors[s] * inverse, 0.0)
    coarse = fac[...].astype(BF16)
    fine = (fac[...] - coarse.astype(F32)).astype(BF16)
    wide = jnp.dot(coarse, held["heads"][...], preferred_element_type=F32) + jnp.dot(
        fine, held["heads"][...], preferred_element_type=F32
    )
    wait(o_all, o_recv)
    summed = wide[0:4] * o_all[0].astype(F32)
    for s in range(1, 16):
        summed = summed + wide[4 * s : 4 * s + 4] * o_all[s].astype(F32)
    attended = (summed * gate[0:4]).astype(BF16)
    out_ref[...] = jnp.dot(attended, woutp[...], preferred_element_type=F32).astype(BF16)

    wait(wg.at[pl.ds(0, 15)], w_send)
    wait(xg.at[pl.ds(0, 31)], x_send)
    wait(kvz.at[pl.ds(0, 15)], kz_send)
    wait(qgb.at[pl.ds(0, 31)], qg_send)
    wait(o_all.at[pl.ds(0, 15)], o_send)
    wait(st_all.at[pl.ds(0, 15)], st_send)
    wait(kvb.at[pl.ds(0, 31)], kv_send)


def shards(
    z_trunk, chain_id, residue, single, gain_single, w_proj, w_out, gain_trunk, w_pair, rel_table, gain_trans,
    w_up, w_down, gain_bias, w_bias,
):
    heads, perm = orders()
    dma = pltpu.SemaphoreType.DMA
    args = {
        "x": single,
        "gain": gain_single.reshape(6, 128),
        "wt": w_proj.T,
        "heads": jnp.asarray(heads, BF16),
        "chain": chain_id.reshape(16, 128),
        "res": residue.reshape(16, 128),
        "gtrunk": gain_trunk.reshape(1, 128),
        "wpair": w_pair,
        "rel": rel_table,
        "gtrans": gain_trans,
        "wup": w_up,
        "wdown": w_down,
        "gbias": gain_bias.reshape(1, 128),
        "wbias": w_bias.T,
        "wout": w_out,
        "perm": jnp.asarray(perm, BF16),
        "z": z_trunk,
        "chain_sm": chain_id,
        "res_sm": residue,
    }
    held = [
        (pltpu.SMEM if name.endswith("_sm") else pltpu.VMEM)(args[name].shape, args[name].dtype) for name in HBM_ARGS
    ]
    return pl.pallas_call(
        main_kernel,
        out_shape=jax.ShapeDtypeStruct((4, 768), BF16),
        in_specs=[pl.BlockSpec(memory_space=pltpu.HBM)] * len(HBM_ARGS),
        out_specs=pl.BlockSpec(memory_space=pltpu.VMEM),
        scratch_shapes=held
        + [
            pltpu.VMEM((4, 768), BF16),
            pltpu.VMEM((32, 4, 768), BF16),
            pltpu.VMEM((16, 6, 768), BF16),
            pltpu.VMEM((128, 768), F32),
            pltpu.VMEM((48, 768), F32),
            pltpu.VMEM((48, 128), BF16),
            pltpu.VMEM((48, 128), BF16),
            pltpu.VMEM((16, 48, 128), BF16),
            pltpu.VMEM((32, 48, 128), BF16),
            pltpu.VMEM((32, 48, 128), BF16),
            pltpu.VMEM((768, 128), BF16),
            pltpu.VMEM((768, 128), BF16),
            pltpu.VMEM((64, 768), F32),
            pltpu.VMEM((1024, 768), BF16),
            pltpu.VMEM((8, 768), F32),
            pltpu.VMEM((1024, 128), F32),
            pltpu.VMEM((768, 768), BF16),
            pltpu.VMEM((16, 4, 768), BF16),
            pltpu.VMEM((16, 4, 768), BF16),
            pltpu.VMEM((16, 8, 128), F32),
            pltpu.VMEM((16, 8, 128), F32),
            pltpu.VMEM((64, 128), F32),
            pltpu.VMEM((128, 128), jnp.int32),
            pltpu.VMEM((128, 128), jnp.int32),
            pltpu.VMEM((128, 256), BF16),
            pltpu.VMEM((2, 512, 128), BF16),
            pltpu.VMEM((2, 128, 256), BF16),
            pltpu.VMEM((16, 128), BF16),
            pltpu.VMEM((128, 128), F32),
            dma((len(HBM_ARGS),)),
            dma, dma((2,)), dma, dma, dma, dma, dma, dma((16,)), dma, dma, dma, dma, dma, dma,
        ],
        compiler_params=pltpu.CompilerParams(
            collective_id=0, has_side_effects=True, vmem_limit_bytes=67043328
        ),
    )(*[args[name] for name in HBM_ARGS])


def solution(mesh):
    return jax.shard_map(
        shards,
        mesh=mesh,
        in_specs=(
            P("row", "col", None), P(), P(), P(("row", "col"), None), P(), P(None, ("row", "col")),
            P(), P(), P(), P(), P(), P(), P(), P(), P(),
        ),
        out_specs=P(("row", "col"), None),
        check_vma=False,
    )
```

```python
import functools

import jax
import jax.numpy as jnp
import numpy as np
from jax import lax
from jax.experimental import pallas as pl
from jax.experimental.pallas import tpu as pltpu
from jax.sharding import PartitionSpec as P

NT = (((1,), (1,)), ((), ()))
F32 = jnp.float32
BF16 = jnp.bfloat16
BIG = 1 << 20
QB = 16
QA = 32
OFFSETS = (1, 0)


def norm_cols(values):
    center = values - jnp.mean(values, axis=0, keepdims=True)
    spread = jnp.mean(center * center, axis=0, keepdims=True)
    return (center * lax.rsqrt(spread + 1e-05)).astype(BF16)


def interval_bounds(chain_k, res_k):
    bins = lax.broadcasted_iota(jnp.int32, (128, 128), 0)
    base = jnp.broadcast_to(chain_k * 64, (128, 128))
    res = jnp.broadcast_to(res_k, (128, 128))
    shifted = res + bins - 32
    inside = (shifted >= 0) & (shifted <= 63)
    low = jnp.where(inside, base + shifted, BIG)
    high = jnp.where(inside, base + shifted, -BIG)

    def put(low, high, index, new_low, new_high):
        hit = bins == index
        return jnp.where(hit, new_low, low), jnp.where(hit, new_high, high)

    low, high = put(low, high, 0, base, base + res - 32)
    low, high = put(low, high, 64, base + res + 32, base + 63)
    low, high = put(low, high, 65, jnp.full_like(base, -BIG), base - 1)
    low, high = put(low, high, 66, base, base + 63)
    low, high = put(low, high, 67, base + 64, base + 127)
    low, high = put(low, high, 68, base + 128, jnp.full_like(base, BIG))
    low, high = put(low, high, 69, jnp.full_like(base, -BIG), base - 65)
    low, high = put(low, high, 70, base + 64, jnp.full_like(base, BIG))
    unused = bins > 70
    return jnp.where(unused, BIG, low), jnp.where(unused, -BIG, high)


def prepare_bias(chain_k, res_k, refs, scratch):
    gtrunk_ref, wpair_ref, rel_ref, gtrans_ref, wup_ref, wdown_ref, gbias_ref, wbias_ref = refs
    low_ref, high_ref, wcat, wup, wdn, wb, rel = scratch
    low, high = interval_bounds(chain_k, res_k)
    low_ref[...] = low
    high_ref[...] = high
    wcat[:, :128] = (wpair_ref[...].astype(F32).T * gtrunk_ref[...]).astype(BF16)
    rel[...] = jnp.zeros_like(rel)
    rel[0:69, :] = rel_ref[0:69, :].astype(F32)
    rel[69:70, :] = rel_ref[64:65, :].astype(F32)
    rel[70:71, :] = rel_ref[65:66, :].astype(F32)
    wcat[:, 128:] = rel[...].T.astype(BF16)
    for t in range(2):
        up = wup_ref[t].astype(F32).T * gtrans_ref[t : t + 1, :]
        wup[t, :256] = (up[:256] * 0.5).astype(BF16)
        wup[t, 256:] = up[256:].astype(BF16)
        wdn[t] = wdown_ref[t].astype(F32).T.astype(BF16)
    wb[...] = (wbias_ref[...].astype(F32) * gbias_ref[...]).astype(BF16)


def bias_block(first, codes, z_ref, scratch, bias):
    low_ref, high_ref, wcat, wup, wdn, wb, _ = scratch
    low = low_ref[...]
    high = high_ref[...]
    tiles = [z_ref[first + j].astype(F32).T for j in range(QB)]
    normed = norm_cols(jnp.concatenate(tiles, axis=1))
    hots = []
    for j in range(QB):
        code = codes(first + j)
        hots.append(jnp.where((low <= code) & (high >= code), 1.0, 0.0).astype(BF16))
    both = jnp.concatenate([normed, jnp.concatenate(hots, axis=1)], axis=0)
    pair = jnp.dot(wcat[...], both, preferred_element_type=F32)
    for t in range(2):
        expanded = jnp.dot(wup[t], norm_cols(pair), preferred_element_type=F32)
        half = expanded[:256]
        product = half * expanded[256:]
        swiglu = (product + product * jnp.tanh(half)).astype(BF16)
        pair = pair + jnp.dot(wdn[t], swiglu, preferred_element_type=F32)
    out = jnp.dot(wb[...], norm_cols(pair), preferred_element_type=F32)
    for j in range(QB):
        bias[pl.ds(pl.multiple_of((first + j) * 16, 16), 16), :] = out[:, j * 128 : (j + 1) * 128]


def orders():
    natural = np.zeros(768, np.int64)
    for g in range(32):
        for zk in range(4):
            for i in range(6):
                natural[g * 24 + zk * 6 + i] = 192 * zk + 6 * g + i
    heads = np.zeros((128, 768), np.float32)
    heads[natural // 48, np.arange(768)] = 1.0
    perm = np.zeros((768, 768), np.float32)
    perm[np.arange(768), natural] = 1.0
    return heads, perm


HBM_ARGS = (
    "x", "gain", "wt", "chain_sm", "res_sm", "chain", "res", "gtrunk", "wpair", "rel", "gtrans", "wup", "wdown", "gbias",
    "wbias", "z", "heads", "wout", "perm",
)


def main_kernel(*refs):
    count = len(HBM_ARGS)
    source = dict(zip(HBM_ARGS, refs[:count]))
    out_ref = refs[count]
    held = dict(zip(HBM_ARGS, refs[count + 1 : 2 * count + 1]))
    (
        xs, xg, wg, xf, wf, kvs, qgs, kvz, kvb, qgb, kt, vt, qf, spread, gate, bias, woutp,
        o_src, o_all, st_src, st_all, fac, low, high, wcat, wup, wdn, wb, rel,
        local_sem, w_send, w_recv, x_send, x_recv, qg_send, qg_recv, kz_send, kz_recv, kv_send, kv_recv,
        o_send, o_recv, st_send, st_recv,
    ) = refs[2 * count + 1 :]
    row_pos = lax.axis_index("row")
    col_pos = lax.axis_index("col")
    z = lax.div(row_pos, 2)
    yh = lax.rem(row_pos, 2)
    g = yh * 16 + col_pos
    middle = lax.rem(lax.div(z + 4, 8), 2)

    def line(zz):
        return {"row": zz * 2 + yh, "col": col_pos}

    def plane(gg):
        return {"row": z * 2 + lax.div(gg, 16), "col": lax.rem(gg, 16)}

    def remote(src, dst, send, recv, device):
        return pltpu.make_async_remote_copy(
            src_ref=src, dst_ref=dst, send_sem=send, recv_sem=recv,
            device_id=device, device_id_type=pl.DeviceIdType.MESH,
        )

    def wait(ref, sem):
        pltpu.make_async_copy(ref, ref, sem).wait()

    def loop(count, body):
        lax.fori_loop(0, count, lambda i, carry: (body(i), carry)[1], 0)

    def far(i):
        return 8 + lax.div(i + 1, 2) * (1 - 2 * lax.rem(i, 2))

    def near(i):
        return lax.rem(16 + lax.div(i + 1, 2) * (1 - 2 * lax.rem(i, 2)), 16)


    loads = {
        name: pltpu.make_async_copy(source[name], held[name], local_sem.at[index])
        for index, name in enumerate(HBM_ARGS)
    }
    barrier = pltpu.get_barrier_semaphore()

    def greet_line(i):
        pl.semaphore_signal(barrier, inc=1, device_id=line(lax.rem(z + 1 + i, 16)), device_id_type=pl.DeviceIdType.MESH)

    def greet_plane(i):
        pl.semaphore_signal(barrier, inc=1, device_id=plane(lax.rem(g + 1 + i, 32)), device_id_type=pl.DeviceIdType.MESH)

    loop(15, greet_line)
    loop(31, greet_plane)
    for name in HBM_ARGS:
        loads[name].start()
    loads["x"].wait()
    loads["gain"].wait()
    x = held["x"][...].astype(F32)
    center = x - jnp.mean(x, axis=-1, keepdims=True)
    deviation = jnp.mean(center * center, axis=-1, keepdims=True)
    gain = jnp.concatenate([held["gain"][k : k + 1, :] for k in range(6)], axis=1)
    xs[...] = (center * lax.rsqrt(deviation + 1e-05) * gain).astype(BF16)
    pair_args = ("gtrunk", "wpair", "rel", "gtrans", "wup", "wdown", "gbias", "wbias")
    for name in ("wt", "heads", "chain", "res", "chain_sm", "res_sm", "z") + pair_args:
        loads[name].wait()
    pair_scratch = (low, high, wcat, wup, wdn, wb, rel)
    prepare_bias(
        held["chain"][pl.ds(col_pos, 1), :], held["res"][pl.ds(col_pos, 1), :],
        [held[name] for name in pair_args], pair_scratch,
    )

    def code_of(index):
        token = row_pos * 64 + index
        return held["chain_sm"][token] * 64 + held["res_sm"][token]

    def blocks(start, count):
        loop(count, lambda i: bias_block((start + i) * QB, code_of, held["z"], pair_scratch, bias))

    ahead = jnp.where(z < 4, 3, jnp.where(z < 8, 1, 0))
    meanwhile = jnp.where(z < 4, 1, 2)
    blocks(0, ahead)
    pl.semaphore_wait(barrier, 46)

    wt = held["wt"]
    loop(15, lambda i: remote(wt, wg.at[z], w_send, w_recv.at[middle], line(lax.rem(z + far(i), 16))).start())
    loop(31, lambda i: remote(xs, xg.at[g], x_send, x_recv, plane(lax.rem(g + 1 + i, 32))).start())
    pltpu.make_async_copy(wt, wg.at[z], w_recv.at[middle]).start()
    pltpu.make_async_copy(xs, xg.at[g], x_recv).start()
    blocks(ahead, meanwhile)
    loads["wout"].wait()
    loads["perm"].wait()
    woutp[...] = jnp.dot(held["perm"][...], held["wout"][...], preferred_element_type=F32).astype(BF16)
    wait(xg, x_recv)
    for s in range(32):
        xf[4 * s : 4 * s + 4, :] = xg[s].astype(F32)
    tokens = xf[...].astype(BF16)
    wait(wg.at[pl.ds(4, 8)], w_recv.at[1])
    for s in range(8):
        wf[6 * s : 6 * s + 6, :] = wg[4 + s].astype(F32)
    kvs[...] = lax.dot_general(wf[...].astype(BF16), tokens, NT, preferred_element_type=F32).astype(BF16)

    loop(15, lambda i: remote(kvs, kvz.at[z], kz_send, kz_recv.at[z], line(lax.rem(z + far(i), 16))).start())
    pltpu.make_async_copy(kvs, kvz.at[z], kz_recv.at[z]).start()
    wait(wg.at[pl.ds(0, 8)], w_recv.at[0])
    for s in range(8):
        wf[6 * s : 6 * s + 6, :] = wg[s if s < 4 else s + 8].astype(F32)
    projected = lax.dot_general(
        wf[...].astype(BF16), xf[...].astype(BF16), NT, preferred_element_type=F32
    )
    qgs[0:24] = projected[0:24].astype(BF16)
    qgs[24:48] = jax.nn.sigmoid(projected[24:48]).astype(BF16)
    loop(31, lambda i: remote(qgs, qgb.at[g], qg_send, qg_recv, plane(lax.rem(g + 1 + i, 32))).start())
    pltpu.make_async_copy(qgs, qgb.at[g], qg_recv).start()
    def forward(i):
        s = lax.rem(z + near(i), 16)
        wait(kvz.at[s], kz_recv.at[s])
        for y in range(2):
            itself = (yh == y) & (col_pos == s)

            @pl.when(itself)
            def _():
                pltpu.make_async_copy(kvz.at[s], kvb.at[g], kv_recv).start()

            @pl.when(jnp.logical_not(itself))
            def _():
                remote(kvz.at[s], kvb.at[g], kv_send, kv_recv, {"row": z * 2 + y, "col": s}).start()

    loop(8, forward)
    blocks(ahead + meanwhile, 64 // QB - ahead - meanwhile)
    wait(qgb, qg_recv)

    def unpack(ref, first):
        return ref[:, first : first + 24, :].astype(F32).reshape(768, 128).astype(BF16)

    rows = lax.broadcasted_iota(jnp.int32, (64, 128), 0)
    lanes = lax.broadcasted_iota(jnp.int32, (64, 128), 1)
    pick = jnp.where(rows + yh * 64 == lanes, 1.0, 0.0).astype(BF16)
    qf[...] = lax.dot_general(pick, unpack(qgb, 0), NT, preferred_element_type=F32)
    mask = held["heads"][0:16, :].astype(F32)

    def spread_queries(i):
        queries = qf[pl.ds(pl.multiple_of(i * 8, 8), 8), :]
        spread[pl.ds(pl.multiple_of(i * 128, 128), 128), :] = (
            (queries[:, None, :] * mask[None]).reshape(128, 768).astype(BF16)
        )

    loop(8, spread_queries)
    rows = lax.broadcasted_iota(jnp.int32, (8, 128), 0)
    lanes = lax.broadcasted_iota(jnp.int32, (8, 128), 1)
    pick = jnp.where((rows + yh * 64 + col_pos * 4 == lanes) & (rows < 4), 1.0, 0.0).astype(BF16)
    gate[...] = lax.dot_general(pick, unpack(qgb, 24), NT, preferred_element_type=F32)


    loop(8, lambda i: forward(i + 8))
    wait(kvb, kv_recv)
    kt[...] = unpack(kvb, 0)
    vt[...] = unpack(kvb, 24)
    rows = lax.broadcasted_iota(jnp.int32, (QA * 16, 128), 0)
    lanes = lax.broadcasted_iota(jnp.int32, (QA * 16, 128), 1)
    own = jnp.where(jnp.bitwise_and(rows, 15) == lanes, 1.0, 0.0)

    def send_parts(d):
        @pl.when(d == col_pos)
        def _():
            pltpu.make_async_copy(o_src.at[d], o_all.at[col_pos], o_recv).start()
            pltpu.make_async_copy(st_src.at[d], st_all.at[col_pos], st_recv).start()

        @pl.when(d != col_pos)
        def _():
            there = {"row": row_pos, "col": d}
            remote(o_src.at[d], o_all.at[col_pos], o_send, o_recv, there).start()
            remote(st_src.at[d], st_all.at[col_pos], st_send, st_recv, there).start()

    def attend(i):
        base = pl.multiple_of(i * (QA * 16), QA * 16)
        scores = jnp.dot(spread[pl.ds(base, QA * 16), :], kt[...], preferred_element_type=F32)
        scores = scores * (48.0**-0.5) + bias[pl.ds(base, QA * 16), :]
        peak = jnp.max(scores, axis=-1, keepdims=True)
        expo = jnp.exp(scores - peak)
        total = jnp.sum(expo, axis=-1, keepdims=True)
        wide = lax.dot_general(expo.astype(BF16), vt[...], NT, preferred_element_type=F32)
        summed = jnp.sum(wide.reshape(QA, 16, 768) * mask[None], axis=1).astype(BF16)
        peaks = jnp.sum((peak * own).reshape(QA, 16, 128), axis=1)
        totals = jnp.sum((total * own).reshape(QA, 16, 128), axis=1)
        for k in range(QA // 4):
            part = i * (QA // 4) + k
            o_src[part] = summed[4 * k : 4 * k + 4]
            st_src[part, 0:4, :] = peaks[4 * k : 4 * k + 4]
            st_src[part, 4:8, :] = totals[4 * k : 4 * k + 4]

    parts = 64 // QA
    first = lax.div(col_pos, QA // 4)
    for offset in OFFSETS:
        block = lax.rem(first + offset, parts)
        attend(block)
        loop(QA // 4, lambda k, block=block: send_parts(block * (QA // 4) + k))
    wait(st_all, st_recv)
    stats = st_all[...]
    peak = stats[0, 0:4]
    for s in range(1, 16):
        peak = jnp.maximum(peak, stats[s, 0:4])
    factors = [jnp.exp(stats[s, 0:4] - peak) for s in range(16)]
    total = factors[0] * stats[0, 4:8]
    for s in range(1, 16):
        total = total + factors[s] * stats[s, 4:8]
    lanes = lax.broadcasted_iota(jnp.int32, (4, 128), 1)
    inverse = 1.0 / jnp.where(lanes < 16, total, 1.0)
    for s in range(16):
        fac[4 * s : 4 * s + 4, :] = jnp.where(lanes < 16, factors[s] * inverse, 0.0)
    coarse = fac[...].astype(BF16)
    fine = (fac[...] - coarse.astype(F32)).astype(BF16)
    wide = jnp.dot(coarse, held["heads"][...], preferred_element_type=F32) + jnp.dot(
        fine, held["heads"][...], preferred_element_type=F32
    )
    wait(o_all, o_recv)
    summed = wide[0:4] * o_all[0].astype(F32)
    for s in range(1, 16):
        summed = summed + wide[4 * s : 4 * s + 4] * o_all[s].astype(F32)
    attended = (summed * gate[0:4]).astype(BF16)
    out_ref[...] = jnp.dot(attended, woutp[...], preferred_element_type=F32).astype(BF16)

    wait(wg.at[pl.ds(0, 15)], w_send)
    wait(xg.at[pl.ds(0, 31)], x_send)
    wait(kvz.at[pl.ds(0, 15)], kz_send)
    wait(qgb.at[pl.ds(0, 31)], qg_send)
    wait(o_all.at[pl.ds(0, 15)], o_send)
    wait(st_all.at[pl.ds(0, 15)], st_send)
    wait(kvb.at[pl.ds(0, 31)], kv_send)


def shards(
    z_trunk, chain_id, residue, single, gain_single, w_proj, w_out, gain_trunk, w_pair, rel_table, gain_trans,
    w_up, w_down, gain_bias, w_bias,
):
    heads, perm = orders()
    dma = pltpu.SemaphoreType.DMA
    args = {
        "x": single,
        "gain": gain_single.reshape(6, 128),
        "wt": w_proj.T,
        "heads": jnp.asarray(heads, BF16),
        "chain": chain_id.reshape(16, 128),
        "res": residue.reshape(16, 128),
        "gtrunk": gain_trunk.reshape(1, 128),
        "wpair": w_pair,
        "rel": rel_table,
        "gtrans": gain_trans,
        "wup": w_up,
        "wdown": w_down,
        "gbias": gain_bias.reshape(1, 128),
        "wbias": w_bias.T,
        "wout": w_out,
        "perm": jnp.asarray(perm, BF16),
        "z": z_trunk,
        "chain_sm": chain_id,
        "res_sm": residue,
    }
    held = [
        (pltpu.SMEM if name.endswith("_sm") else pltpu.VMEM)(args[name].shape, args[name].dtype) for name in HBM_ARGS
    ]
    return pl.pallas_call(
        main_kernel,
        out_shape=jax.ShapeDtypeStruct((4, 768), BF16),
        in_specs=[pl.BlockSpec(memory_space=pltpu.HBM)] * len(HBM_ARGS),
        out_specs=pl.BlockSpec(memory_space=pltpu.VMEM),
        scratch_shapes=held
        + [
            pltpu.VMEM((4, 768), BF16),
            pltpu.VMEM((32, 4, 768), BF16),
            pltpu.VMEM((16, 6, 768), BF16),
            pltpu.VMEM((128, 768), F32),
            pltpu.VMEM((48, 768), F32),
            pltpu.VMEM((48, 128), BF16),
            pltpu.VMEM((48, 128), BF16),
            pltpu.VMEM((16, 48, 128), BF16),
            pltpu.VMEM((32, 48, 128), BF16),
            pltpu.VMEM((32, 48, 128), BF16),
            pltpu.VMEM((768, 128), BF16),
            pltpu.VMEM((768, 128), BF16),
            pltpu.VMEM((64, 768), F32),
            pltpu.VMEM((1024, 768), BF16),
            pltpu.VMEM((8, 768), F32),
            pltpu.VMEM((1024, 128), F32),
            pltpu.VMEM((768, 768), BF16),
            pltpu.VMEM((16, 4, 768), BF16),
            pltpu.VMEM((16, 4, 768), BF16),
            pltpu.VMEM((16, 8, 128), F32),
            pltpu.VMEM((16, 8, 128), F32),
            pltpu.VMEM((64, 128), F32),
            pltpu.VMEM((128, 128), jnp.int32),
            pltpu.VMEM((128, 128), jnp.int32),
            pltpu.VMEM((128, 256), BF16),
            pltpu.VMEM((2, 512, 128), BF16),
            pltpu.VMEM((2, 128, 256), BF16),
            pltpu.VMEM((16, 128), BF16),
            pltpu.VMEM((128, 128), F32),
            dma((len(HBM_ARGS),)),
            dma, dma((2,)), dma, dma, dma, dma, dma, dma((16,)), dma, dma, dma, dma, dma, dma,
        ],
        compiler_params=pltpu.CompilerParams(
            collective_id=0, has_side_effects=True, vmem_limit_bytes=67043328
        ),
    )(*[args[name] for name in HBM_ARGS])


def solution(mesh):
    return jax.shard_map(
        shards,
        mesh=mesh,
        in_specs=(
            P("row", "col", None), P(), P(), P(("row", "col"), None), P(), P(None, ("row", "col")),
            P(), P(), P(), P(), P(), P(), P(), P(), P(),
        ),
        out_specs=P(("row", "col"), None),
        check_vma=False,
    )
```

```python
import functools

import jax
import jax.numpy as jnp
import numpy as np
from jax import lax
from jax.experimental import pallas as pl
from jax.experimental.pallas import tpu as pltpu
from jax.sharding import PartitionSpec as P

NT = (((1,), (1,)), ((), ()))
F32 = jnp.float32
BF16 = jnp.bfloat16
BIG = 1 << 20
QB = 16
QA = 32
OFFSETS = (1, 0)


def norm_cols(values):
    center = values - jnp.mean(values, axis=0, keepdims=True)
    spread = jnp.mean(center * center, axis=0, keepdims=True)
    return (center * lax.rsqrt(spread + 1e-05)).astype(BF16)


def interval_bounds(chain_k, res_k):
    bins = lax.broadcasted_iota(jnp.int32, (128, 128), 0)
    base = jnp.broadcast_to(chain_k * 64, (128, 128))
    res = jnp.broadcast_to(res_k, (128, 128))
    shifted = res + bins - 32
    inside = (shifted >= 0) & (shifted <= 63)
    low = jnp.where(inside, base + shifted, BIG)
    high = jnp.where(inside, base + shifted, -BIG)

    def put(low, high, index, new_low, new_high):
        hit = bins == index
        return jnp.where(hit, new_low, low), jnp.where(hit, new_high, high)

    low, high = put(low, high, 0, base, base + res - 32)
    low, high = put(low, high, 64, base + res + 32, base + 63)
    low, high = put(low, high, 65, jnp.full_like(base, -BIG), base - 1)
    low, high = put(low, high, 66, base, base + 63)
    low, high = put(low, high, 67, base + 64, base + 127)
    low, high = put(low, high, 68, base + 128, jnp.full_like(base, BIG))
    low, high = put(low, high, 69, jnp.full_like(base, -BIG), base - 65)
    low, high = put(low, high, 70, base + 64, jnp.full_like(base, BIG))
    unused = bins > 70
    return jnp.where(unused, BIG, low), jnp.where(unused, -BIG, high)


def prepare_bias(chain_k, res_k, refs, scratch):
    gtrunk_ref, wpair_ref, rel_ref, gtrans_ref, wup_ref, wdown_ref, gbias_ref, wbias_ref = refs
    low_ref, high_ref, wcat, wup, wdn, wb, rel = scratch
    low, high = interval_bounds(chain_k, res_k)
    low_ref[...] = low
    high_ref[...] = high
    wcat[:, :128] = (wpair_ref[...].astype(F32).T * gtrunk_ref[...]).astype(BF16)
    rel[...] = jnp.zeros_like(rel)
    rel[0:69, :] = rel_ref[0:69, :].astype(F32)
    rel[69:70, :] = rel_ref[64:65, :].astype(F32)
    rel[70:71, :] = rel_ref[65:66, :].astype(F32)
    wcat[:, 128:] = rel[...].T.astype(BF16)
    for t in range(2):
        up = wup_ref[t].astype(F32).T * gtrans_ref[t : t + 1, :]
        wup[t, :256] = (up[:256] * 0.5).astype(BF16)
        wup[t, 256:] = up[256:].astype(BF16)
        wdn[t] = wdown_ref[t].astype(F32).T.astype(BF16)
    wb[...] = (wbias_ref[...].astype(F32) * gbias_ref[...]).astype(BF16)


def bias_block(first, codes, z_ref, scratch, bias):
    low_ref, high_ref, wcat, wup, wdn, wb, _ = scratch
    low = low_ref[...]
    high = high_ref[...]
    tiles = [z_ref[first + j].astype(F32).T for j in range(QB)]
    normed = norm_cols(jnp.concatenate(tiles, axis=1))
    hots = []
    for j in range(QB):
        code = codes(first + j)
        hots.append(jnp.where((low <= code) & (high >= code), 1.0, 0.0).astype(BF16))
    both = jnp.concatenate([normed, jnp.concatenate(hots, axis=1)], axis=0)
    pair = jnp.dot(wcat[...], both, preferred_element_type=F32)
    for t in range(2):
        expanded = jnp.dot(wup[t], norm_cols(pair), preferred_element_type=F32)
        half = expanded[:256]
        product = half * expanded[256:]
        swiglu = (product + product * jnp.tanh(half)).astype(BF16)
        pair = pair + jnp.dot(wdn[t], swiglu, preferred_element_type=F32)
    out = jnp.dot(wb[...], norm_cols(pair), preferred_element_type=F32)
    for j in range(QB):
        bias[pl.ds(pl.multiple_of((first + j) * 16, 16), 16), :] = out[:, j * 128 : (j + 1) * 128]


def orders():
    natural = np.zeros(768, np.int64)
    for g in range(32):
        for zk in range(4):
            for i in range(6):
                natural[g * 24 + zk * 6 + i] = 192 * zk + 6 * g + i
    heads = np.zeros((128, 768), np.float32)
    heads[natural // 48, np.arange(768)] = 1.0
    perm = np.zeros((768, 768), np.float32)
    perm[np.arange(768), natural] = 1.0
    return heads, perm


HBM_ARGS = (
    "x", "gain", "wt", "chain_sm", "res_sm", "chain", "res", "gtrunk", "wpair", "rel", "gtrans", "wup", "wdown", "gbias",
    "wbias", "z", "heads", "wout", "perm",
)


def main_kernel(*refs):
    count = len(HBM_ARGS)
    source = dict(zip(HBM_ARGS, refs[:count]))
    out_ref = refs[count]
    held = dict(zip(HBM_ARGS, refs[count + 1 : 2 * count + 1]))
    (
        xs, xg, wg, xf, wf, kvs, qgs, kvz, kvb, qgb, kt, vt, qf, spread, gate, bias, woutp,
        o_src, o_all, st_src, st_all, fac, low, high, wcat, wup, wdn, wb, rel,
        local_sem, w_send, w_recv, x_send, x_recv, qg_send, qg_recv, kz_send, kz_recv, kv_send, kv_recv,
        o_send, o_recv, st_send, st_recv,
    ) = refs[2 * count + 1 :]
    row_pos = lax.axis_index("row")
    col_pos = lax.axis_index("col")
    z = lax.div(row_pos, 2)
    yh = lax.rem(row_pos, 2)
    g = yh * 16 + col_pos
    middle = lax.rem(lax.div(z + 4, 8), 2)

    def line(zz):
        return {"row": zz * 2 + yh, "col": col_pos}

    def plane(gg):
        return {"row": z * 2 + lax.div(gg, 16), "col": lax.rem(gg, 16)}

    def remote(src, dst, send, recv, device):
        return pltpu.make_async_remote_copy(
            src_ref=src, dst_ref=dst, send_sem=send, recv_sem=recv,
            device_id=device, device_id_type=pl.DeviceIdType.MESH,
        )

    def wait(ref, sem):
        pltpu.make_async_copy(ref, ref, sem).wait()

    def loop(count, body):
        lax.fori_loop(0, count, lambda i, carry: (body(i), carry)[1], 0)

    def far(i):
        return 8 + lax.div(i + 1, 2) * (1 - 2 * lax.rem(i, 2))

    def near(i):
        return lax.rem(16 + lax.div(i + 1, 2) * (1 - 2 * lax.rem(i, 2)), 16)


    loads = {
        name: pltpu.make_async_copy(source[name], held[name], local_sem.at[index])
        for index, name in enumerate(HBM_ARGS)
    }
    barrier = pltpu.get_barrier_semaphore()

    def greet_line(i):
        pl.semaphore_signal(barrier, inc=1, device_id=line(lax.rem(z + 1 + i, 16)), device_id_type=pl.DeviceIdType.MESH)

    def greet_plane(i):
        pl.semaphore_signal(barrier, inc=1, device_id=plane(lax.rem(g + 1 + i, 32)), device_id_type=pl.DeviceIdType.MESH)

    loop(15, greet_line)
    loop(31, greet_plane)
    for name in HBM_ARGS:
        loads[name].start()
    loads["x"].wait()
    loads["gain"].wait()
    x = held["x"][...].astype(F32)
    center = x - jnp.mean(x, axis=-1, keepdims=True)
    deviation = jnp.mean(center * center, axis=-1, keepdims=True)
    gain = jnp.concatenate([held["gain"][k : k + 1, :] for k in range(6)], axis=1)
    xs[...] = (center * lax.rsqrt(deviation + 1e-05) * gain).astype(BF16)
    pair_args = ("gtrunk", "wpair", "rel", "gtrans", "wup", "wdown", "gbias", "wbias")
    for name in ("wt", "heads", "chain", "res", "chain_sm", "res_sm", "z") + pair_args:
        loads[name].wait()
    pair_scratch = (low, high, wcat, wup, wdn, wb, rel)
    prepare_bias(
        held["chain"][pl.ds(col_pos, 1), :], held["res"][pl.ds(col_pos, 1), :],
        [held[name] for name in pair_args], pair_scratch,
    )

    def code_of(index):
        token = row_pos * 64 + index
        return held["chain_sm"][token] * 64 + held["res_sm"][token]

    def blocks(start, count):
        loop(count, lambda i: bias_block((start + i) * QB, code_of, held["z"], pair_scratch, bias))

    ahead = jnp.where(z < 4, 3, jnp.where(z < 8, 1, 0))
    meanwhile = jnp.where(z < 4, 1, 2)
    blocks(0, ahead)
    pl.semaphore_wait(barrier, 46)

    wt = held["wt"]
    loop(15, lambda i: remote(wt, wg.at[z], w_send, w_recv.at[middle], line(lax.rem(z + far(i), 16))).start())
    loop(31, lambda i: remote(xs, xg.at[g], x_send, x_recv, plane(lax.rem(g + 1 + i, 32))).start())
    pltpu.make_async_copy(wt, wg.at[z], w_recv.at[middle]).start()
    pltpu.make_async_copy(xs, xg.at[g], x_recv).start()
    blocks(ahead, meanwhile)
    loads["wout"].wait()
    loads["perm"].wait()
    woutp[...] = jnp.dot(held["perm"][...], held["wout"][...], preferred_element_type=F32).astype(BF16)
    wait(xg, x_recv)
    for s in range(32):
        xf[4 * s : 4 * s + 4, :] = xg[s].astype(F32)
    tokens = xf[...].astype(BF16)
    wait(wg.at[pl.ds(4, 8)], w_recv.at[1])
    for s in range(8):
        wf[6 * s : 6 * s + 6, :] = wg[4 + s].astype(F32)
    kvs[...] = lax.dot_general(wf[...].astype(BF16), tokens, NT, preferred_element_type=F32).astype(BF16)

    loop(15, lambda i: remote(kvs, kvz.at[z], kz_send, kz_recv.at[z], line(lax.rem(z + far(i), 16))).start())
    pltpu.make_async_copy(kvs, kvz.at[z], kz_recv.at[z]).start()
    wait(wg.at[pl.ds(0, 8)], w_recv.at[0])
    for s in range(8):
        wf[6 * s : 6 * s + 6, :] = wg[s if s < 4 else s + 8].astype(F32)
    projected = lax.dot_general(
        wf[...].astype(BF16), xf[...].astype(BF16), NT, preferred_element_type=F32
    )
    qgs[0:24] = projected[0:24].astype(BF16)
    qgs[24:48] = jax.nn.sigmoid(projected[24:48]).astype(BF16)
    loop(31, lambda i: remote(qgs, qgb.at[g], qg_send, qg_recv, plane(lax.rem(g + 1 + i, 32))).start())
    pltpu.make_async_copy(qgs, qgb.at[g], qg_recv).start()
    def forward(i):
        s = lax.rem(z + near(i), 16)
        wait(kvz.at[s], kz_recv.at[s])
        for y in range(2):
            itself = (yh == y) & (col_pos == s)

            @pl.when(itself)
            def _():
                pltpu.make_async_copy(kvz.at[s], kvb.at[g], kv_recv).start()

            @pl.when(jnp.logical_not(itself))
            def _():
                remote(kvz.at[s], kvb.at[g], kv_send, kv_recv, {"row": z * 2 + y, "col": s}).start()

    loop(8, forward)
    blocks(ahead + meanwhile, 64 // QB - ahead - meanwhile)
    wait(qgb, qg_recv)

    def unpack(ref, first):
        return ref[:, first : first + 24, :].astype(F32).reshape(768, 128).astype(BF16)

    rows = lax.broadcasted_iota(jnp.int32, (64, 128), 0)
    lanes = lax.broadcasted_iota(jnp.int32, (64, 128), 1)
    pick = jnp.where(rows + yh * 64 == lanes, 1.0, 0.0).astype(BF16)
    qf[...] = lax.dot_general(pick, unpack(qgb, 0), NT, preferred_element_type=F32)
    mask = held["heads"][0:16, :].astype(F32)

    def spread_queries(i):
        queries = qf[pl.ds(pl.multiple_of(i * 8, 8), 8), :]
        spread[pl.ds(pl.multiple_of(i * 128, 128), 128), :] = (
            (queries[:, None, :] * mask[None]).reshape(128, 768).astype(BF16)
        )

    loop(8, spread_queries)
    rows = lax.broadcasted_iota(jnp.int32, (8, 128), 0)
    lanes = lax.broadcasted_iota(jnp.int32, (8, 128), 1)
    pick = jnp.where((rows + yh * 64 + col_pos * 4 == lanes) & (rows < 4), 1.0, 0.0).astype(BF16)
    gate[...] = lax.dot_general(pick, unpack(qgb, 24), NT, preferred_element_type=F32)


    loop(8, lambda i: forward(i + 8))
    wait(kvb, kv_recv)
    kt[...] = unpack(kvb, 0)
    vt[...] = unpack(kvb, 24)
    rows = lax.broadcasted_iota(jnp.int32, (QA * 16, 128), 0)
    lanes = lax.broadcasted_iota(jnp.int32, (QA * 16, 128), 1)
    own = jnp.where(jnp.bitwise_and(rows, 15) == lanes, 1.0, 0.0)

    def send_part(src, dst, send, recv, d):
        @pl.when(d == col_pos)
        def _():
            pltpu.make_async_copy(src.at[d], dst.at[col_pos], recv).start()

        @pl.when(d != col_pos)
        def _():
            remote(src.at[d], dst.at[col_pos], send, recv, {"row": row_pos, "col": d}).start()

    def attend(i):
        base = pl.multiple_of(i * (QA * 16), QA * 16)
        scores = jnp.dot(spread[pl.ds(base, QA * 16), :], kt[...], preferred_element_type=F32)
        scores = scores * (48.0**-0.5) + bias[pl.ds(base, QA * 16), :]
        peak = jnp.max(scores, axis=-1, keepdims=True)
        expo = jnp.exp(scores - peak)
        total = jnp.sum(expo, axis=-1, keepdims=True)
        peaks = jnp.sum((peak * own).reshape(QA, 16, 128), axis=1)
        totals = jnp.sum((total * own).reshape(QA, 16, 128), axis=1)
        for k in range(QA // 4):
            part = i * (QA // 4) + k
            st_src[part, 0:4, :] = peaks[4 * k : 4 * k + 4]
            st_src[part, 4:8, :] = totals[4 * k : 4 * k + 4]
        loop(QA // 4, lambda k: send_part(st_src, st_all, st_send, st_recv, i * (QA // 4) + k))
        wide = lax.dot_general(expo.astype(BF16), vt[...], NT, preferred_element_type=F32)
        summed = jnp.sum(wide.reshape(QA, 16, 768) * mask[None], axis=1).astype(BF16)
        for k in range(QA // 4):
            o_src[i * (QA // 4) + k] = summed[4 * k : 4 * k + 4]
        loop(QA // 4, lambda k: send_part(o_src, o_all, o_send, o_recv, i * (QA // 4) + k))

    parts = 64 // QA
    first = lax.div(col_pos, QA // 4)
    for offset in OFFSETS:
        attend(lax.rem(first + offset, parts))
    wait(st_all, st_recv)
    stats = st_all[...]
    peak = stats[0, 0:4]
    for s in range(1, 16):
        peak = jnp.maximum(peak, stats[s, 0:4])
    factors = [jnp.exp(stats[s, 0:4] - peak) for s in range(16)]
    total = factors[0] * stats[0, 4:8]
    for s in range(1, 16):
        total = total + factors[s] * stats[s, 4:8]
    lanes = lax.broadcasted_iota(jnp.int32, (4, 128), 1)
    inverse = 1.0 / jnp.where(lanes < 16, total, 1.0)
    for s in range(16):
        fac[4 * s : 4 * s + 4, :] = jnp.where(lanes < 16, factors[s] * inverse, 0.0)
    coarse = fac[...].astype(BF16)
    fine = (fac[...] - coarse.astype(F32)).astype(BF16)
    wide = jnp.dot(coarse, held["heads"][...], preferred_element_type=F32) + jnp.dot(
        fine, held["heads"][...], preferred_element_type=F32
    )
    wait(o_all, o_recv)
    summed = wide[0:4] * o_all[0].astype(F32)
    for s in range(1, 16):
        summed = summed + wide[4 * s : 4 * s + 4] * o_all[s].astype(F32)
    attended = (summed * gate[0:4]).astype(BF16)
    out_ref[...] = jnp.dot(attended, woutp[...], preferred_element_type=F32).astype(BF16)

    wait(wg.at[pl.ds(0, 15)], w_send)
    wait(xg.at[pl.ds(0, 31)], x_send)
    wait(kvz.at[pl.ds(0, 15)], kz_send)
    wait(qgb.at[pl.ds(0, 31)], qg_send)
    wait(o_all.at[pl.ds(0, 15)], o_send)
    wait(st_all.at[pl.ds(0, 15)], st_send)
    wait(kvb.at[pl.ds(0, 31)], kv_send)


def shards(
    z_trunk, chain_id, residue, single, gain_single, w_proj, w_out, gain_trunk, w_pair, rel_table, gain_trans,
    w_up, w_down, gain_bias, w_bias,
):
    heads, perm = orders()
    dma = pltpu.SemaphoreType.DMA
    args = {
        "x": single,
        "gain": gain_single.reshape(6, 128),
        "wt": w_proj.T,
        "heads": jnp.asarray(heads, BF16),
        "chain": chain_id.reshape(16, 128),
        "res": residue.reshape(16, 128),
        "gtrunk": gain_trunk.reshape(1, 128),
        "wpair": w_pair,
        "rel": rel_table,
        "gtrans": gain_trans,
        "wup": w_up,
        "wdown": w_down,
        "gbias": gain_bias.reshape(1, 128),
        "wbias": w_bias.T,
        "wout": w_out,
        "perm": jnp.asarray(perm, BF16),
        "z": z_trunk,
        "chain_sm": chain_id,
        "res_sm": residue,
    }
    held = [
        (pltpu.SMEM if name.endswith("_sm") else pltpu.VMEM)(args[name].shape, args[name].dtype) for name in HBM_ARGS
    ]
    return pl.pallas_call(
        main_kernel,
        out_shape=jax.ShapeDtypeStruct((4, 768), BF16),
        in_specs=[pl.BlockSpec(memory_space=pltpu.HBM)] * len(HBM_ARGS),
        out_specs=pl.BlockSpec(memory_space=pltpu.VMEM),
        scratch_shapes=held
        + [
            pltpu.VMEM((4, 768), BF16),
            pltpu.VMEM((32, 4, 768), BF16),
            pltpu.VMEM((16, 6, 768), BF16),
            pltpu.VMEM((128, 768), F32),
            pltpu.VMEM((48, 768), F32),
            pltpu.VMEM((48, 128), BF16),
            pltpu.VMEM((48, 128), BF16),
            pltpu.VMEM((16, 48, 128), BF16),
            pltpu.VMEM((32, 48, 128), BF16),
            pltpu.VMEM((32, 48, 128), BF16),
            pltpu.VMEM((768, 128), BF16),
            pltpu.VMEM((768, 128), BF16),
            pltpu.VMEM((64, 768), F32),
            pltpu.VMEM((1024, 768), BF16),
            pltpu.VMEM((8, 768), F32),
            pltpu.VMEM((1024, 128), F32),
            pltpu.VMEM((768, 768), BF16),
            pltpu.VMEM((16, 4, 768), BF16),
            pltpu.VMEM((16, 4, 768), BF16),
            pltpu.VMEM((16, 8, 128), F32),
            pltpu.VMEM((16, 8, 128), F32),
            pltpu.VMEM((64, 128), F32),
            pltpu.VMEM((128, 128), jnp.int32),
            pltpu.VMEM((128, 128), jnp.int32),
            pltpu.VMEM((128, 256), BF16),
            pltpu.VMEM((2, 512, 128), BF16),
            pltpu.VMEM((2, 128, 256), BF16),
            pltpu.VMEM((16, 128), BF16),
            pltpu.VMEM((128, 128), F32),
            dma((len(HBM_ARGS),)),
            dma, dma((2,)), dma, dma, dma, dma, dma, dma((16,)), dma, dma, dma, dma, dma, dma,
        ],
        compiler_params=pltpu.CompilerParams(
            collective_id=0, has_side_effects=True, vmem_limit_bytes=67043328
        ),
    )(*[args[name] for name in HBM_ARGS])


def solution(mesh):
    return jax.shard_map(
        shards,
        mesh=mesh,
        in_specs=(
            P("row", "col", None), P(), P(), P(("row", "col"), None), P(), P(None, ("row", "col")),
            P(), P(), P(), P(), P(), P(), P(), P(), P(),
        ),
        out_specs=P(("row", "col"), None),
        check_vma=False,
    )
```
